32 devices in a mesh: member: 2 (over x), tile: 16 (over z, y, core).
Axes of the slice: x: 2, y: 2, z: 4, core: 2. Of those that a mesh axis runs over, the one named last changes fastest.
Arguments:
- precip: float32 [1024, 128], P(('member', 'tile')), parts along dimension 0, may hold values from 0.2 to 2
- pet: float32 [1024, 128], P(('member', 'tile')), parts along dimension 0, may hold values from 0.05 to 0.5
- soil_init: float32 [1024, 128], P(('member', 'tile')), parts along dimension 0, may hold values from 0.05 to 0.4
- ksat: float32 [1024, 128], P(('member', 'tile')), parts along dimension 0, may hold values from 0.5 to 3
- land_mask: int32 [1024, 128], P(('member', 'tile')), parts along dimension 0, may hold values 0 or 1
- head_init: float32 [1024, 2048], P(('member', 'tile')), parts along dimension 0, may hold values from 0.2 to 2
- subsurface_init: float32 [1024, 2048], P(('member', 'tile')), parts along dimension 0, may hold values from 0.2 to 2
- conduct: float32 [1024, 2048], P(('member', 'tile')), parts along dimension 0, may hold values from 0.22 to 0.47
- drain_rate: float32 [1024, 2048], P(('member', 'tile')), parts along dimension 0, may hold values from 0.05 to 0.4
- flow_code: int32 [1024, 2048], P(('member', 'tile')), parts along dimension 0, may hold values from 0 to 3
- channel_share: float32 [1024, 2048], P(('member', 'tile')), parts along dimension 0, may hold values from 0.02 to 0.2
- cell_slot: int32 [1024, 2048], P(('member', 'tile')), parts along dimension 0, may hold values from 0 to 1023
- slot_reach: int32 [32768], P(('member', 'tile')), parts along dimension 0, may hold values from 0 to 1023
Outputs:
- soil: float32 [1024, 128], P(('member', 'tile')), parts along dimension 0
- head: float32 [1024, 2048], P(('member', 'tile')), parts along dimension 0
- subsurface: float32 [1024, 2048], P(('member', 'tile')), parts along dimension 0
- reach_inflow: float32 [32768], P(('member', 'tile')), parts along dimension 0
The draws below stay inside these ranges and needn't reach their ends.
There are 2 independent parts, one for each index of `member`. The reference program is written for one: setup_inputs(seed, part) draws one part's arguments, and reference() takes and returns one part's arrays. A program takes and returns all parts, laid end to end along the dimension named above; each array names one. Nothing has to cross between parts.
Inputs may be any that keep to these rules, and one draw needn't show every extreme that they name: `slot_reach`: slot k of a tile holds a reach owned by tile index k // 64.
All inputs are finite; a program needn't handle non-finite values. No bound on the sum of `land_mask` on one device may be relied on, other than what follows from the above.
Results may differ from the reference program's by a relative error of at most 0.00002.
Values sent between devices are 32-bit elements; how exact they have to be, the bound alone decides.
A program may use at most 64 MiB of HBM per device.

```python
import math
import jax
import jax.numpy as jnp

FR_DEV = 32
FC = 2048
ITERS = 6
PER_OWNER = 64
REACH_DEV = 1024
FR = 512
CC = 512
CR = 128
SLOTS = 1024
N_TILE = 16


def set_ends(entries, key, least, largest):
    dims = entries.shape
    spot = [jax.random.randint(jax.random.fold_in(key, axis), (), 0, dims[axis]) for axis in range(len(dims))]
    entries = entries.at[tuple(spot)].set(least)
    longest = dims.index(max(dims))
    spot[longest] = (spot[longest] + 1) % dims[longest]
    return entries.at[tuple(spot)].set(largest)


def shard_levels(stream_key, extent, shards, least, largest):
    gain, own = 1.0, jax.random.fold_in(stream_key, 6)
    for position, blocks in shards:
        steps = jnp.exp(jax.random.uniform(jax.random.fold_in(own, position), (blocks,), jnp.float32, least / len(shards), largest / len(shards)))
        gain = gain * jnp.repeat(steps, extent[position] // blocks).reshape([-1 if axis == position else 1 for axis in range(len(extent))])
    return gain


def setup_inputs(seed: int = 0, part: int = 0) -> dict:
    keys = jax.random.split(jax.random.key(seed), 14)
    part_keys = jax.random.split(jax.random.fold_in(keys[13], part), 14)
    return {
        "precip": jnp.clip(jnp.exp(math.log(2.0) - 2.3025851 * jax.random.uniform(part_keys[0], (CC, CR), jnp.float32) ** shard_levels(part_keys[0], (CC, CR), ((0, 16),), -0.2, 0.2)), 0.2, 2.0),
        "pet": jnp.clip(jnp.exp(math.log(0.5) - 2.3025851 * jax.random.uniform(part_keys[1], (CC, CR), jnp.float32) ** shard_levels(part_keys[1], (CC, CR), ((0, 16),), -0.2, 0.2)), 0.05, 0.5),
        "soil_init": jnp.clip(0.05 + 0.35 * jax.random.uniform(part_keys[2], (CC, CR), jnp.float32) ** shard_levels(part_keys[2], (CC, CR), ((0, 16),), -0.2, 0.2), 0.05, 0.4),
        "ksat": jnp.clip(jnp.exp(math.log(3.0) - 1.7917595 * jax.random.uniform(part_keys[3], (CC, CR), jnp.float32) ** shard_levels(part_keys[3], (CC, CR), ((0, 16),), -0.2, 0.2)), 0.5, 3.0),
        "land_mask": set_ends((jax.random.randint(part_keys[4], (CC, CR), 0, 4) < 3).astype(jnp.int32), jax.random.fold_in(part_keys[4], 1), 0, 1),
        "head_init": jnp.clip(jnp.exp(math.log(2.0) - 2.3025851 * jax.random.uniform(part_keys[5], (FR, FC), jnp.float32) ** shard_levels(part_keys[5], (FR, FC), ((0, 16),), -0.2, 0.2)), 0.2, 2.0),
        "subsurface_init": jnp.clip(jnp.exp(math.log(2.0) - 2.3025851 * jax.random.uniform(part_keys[6], (FR, FC), jnp.float32) ** shard_levels(part_keys[6], (FR, FC), ((0, 16),), -0.2, 0.2)), 0.2, 2.0),
        "conduct": jnp.clip(jnp.exp(math.log(0.47) - 0.75910515 * jax.random.uniform(part_keys[7], (FR, FC), jnp.float32) ** shard_levels(part_keys[7], (FR, FC), ((0, 16),), -0.2, 0.2)), 0.22, 0.47),
        "drain_rate": jnp.clip(jnp.exp(math.log(0.4) - 2.0794415 * jax.random.uniform(part_keys[8], (FR, FC), jnp.float32) ** shard_levels(part_keys[8], (FR, FC), ((0, 16),), -0.2, 0.2)), 0.05, 0.4),
        "flow_code": set_ends(jax.random.randint(part_keys[9], (FR, FC), 0, 4), jax.random.fold_in(part_keys[9], 1), 0, 3).astype(jnp.int32),
        "channel_share": jnp.clip(0.02 + 0.18 * jax.random.uniform(part_keys[10], (FR, FC), jnp.float32) ** shard_levels(part_keys[10], (FR, FC), ((0, 16),), -0.2, 0.2), 0.02, 0.2),
        "cell_slot": set_ends(jax.random.randint(part_keys[11], (FR, FC), 0, SLOTS), jax.random.fold_in(part_keys[11], 1), 0, SLOTS - 1).astype(jnp.int32),
        "slot_reach": set_ends(jax.random.randint(part_keys[12], (N_TILE * SLOTS,), 0, REACH_DEV), jax.random.fold_in(part_keys[12], 1), 0, REACH_DEV - 1).astype(jnp.int32),
    }


def land_step(precip, pet, soil_init, ksat, land_mask):
    mask = land_mask.astype(jnp.float32)
    wet = 2.0 * soil_init
    cap = ksat * (1.0 - wet)
    runoff = mask * precip * precip / (precip + cap)
    drainage = 0.25 * mask * ksat * wet ** 4
    evap = mask * pet * wet
    soil = soil_init + 0.1 * (mask * precip - runoff - drainage - evap)
    return soil, runoff, drainage


def advance(state, statics):
    h = state[0]
    s = state[1]
    g, down, up, right, left = statics[0], statics[1], statics[2], statics[3], statics[4]
    hc = h[1:-1]
    gc = g[1:-1]
    sc = s[1:-1]
    hs = jnp.pad(hc, ((0, 0), (1, 1)))
    gs = jnp.pad(gc, ((0, 0), (1, 1)))
    flux = g[:-2] * (h[:-2] - hc) + g[2:] * (h[2:] - hc)
    flux = flux + gs[:, :-2] * (hs[:, :-2] - hc) + gs[:, 2:] * (hs[:, 2:] - hc)
    h_new = hc + gc * flux
    moving_right = jnp.pad((right * s)[1:-1], ((0, 0), (1, 1)))
    moving_left = jnp.pad((left * s)[1:-1], ((0, 0), (1, 1)))
    incoming = (down * s)[:-2] + (up * s)[2:] + moving_right[:, :-2] + moving_left[:, 2:]
    outgoing = (down + up + right + left)[1:-1]
    s_new = sc - outgoing * sc + incoming
    return jnp.stack([h_new, s_new])


def make_statics(conduct, drain_rate, flow_code):
    parts = [conduct]
    for code in range(4):
        parts.append(drain_rate * (flow_code == code).astype(jnp.float32))
    return jnp.stack(parts)


def reference(precip, pet, soil_init, ksat, land_mask, head_init, subsurface_init, conduct, drain_rate, flow_code, channel_share, cell_slot, slot_reach):
    soil, runoff, drainage = land_step(precip, pet, soil_init, ksat, land_mask)
    fine = jnp.stack([runoff.T, drainage.T])
    fine = jnp.repeat(jnp.repeat(fine, 4, axis=1), 4, axis=2)
    state = jnp.stack([head_init + fine[0], subsurface_init + fine[1]])
    statics = jnp.pad(make_statics(conduct, drain_rate, flow_code), ((0, 0), (1, 1), (0, 0)))
    for step in range(ITERS):
        state = advance(jnp.pad(state, ((0, 0), (1, 1), (0, 0))), statics)
    h = state[0]
    inflow = channel_share * h
    head = h - inflow
    rows = jnp.arange(FR, dtype=jnp.int32) // FR_DEV
    slots = PER_OWNER * N_TILE
    place = slot_reach[(rows[:, None] * slots + cell_slot).astype(jnp.int32)]
    reach_id = (cell_slot // PER_OWNER) * REACH_DEV + place
    reach_inflow = jax.ops.segment_sum(inflow.ravel(), reach_id.ravel().astype(jnp.int32), num_segments=REACH_DEV * N_TILE)
    return soil, head, state[1], reach_inflow
```

```python
import functools

import jax
import jax.numpy as jnp
from jax import lax
from jax.experimental import pallas as pl
from jax.experimental.pallas import tpu as pltpu
from jax.sharding import PartitionSpec as P

ITERS = 6
HALO = 8
TILE = 8
LANES = 128
MESH = pl.DeviceIdType.MESH
NT = (((1,), (1,)), ((), ()))


def parts_of(x, count):
    parts = []
    for _ in range(count):
        part = x.astype(jnp.bfloat16)
        parts.append(part)
        x = x - part.astype(jnp.float32)
    return parts


def kernel(
    n,
    precip,
    pet,
    soil_init,
    ksat,
    land_mask,
    head_init,
    subsurface_init,
    conduct,
    drain_rate,
    flow_code,
    channel_share,
    cell_slot,
    slot_reach,
    soil_out,
    head_out,
    sub_out,
    reach_out,
    land_in,
    mask_in,
    pack,
    land_send,
    land_recv,
    wide,
    h,
    s,
    g,
    d,
    code,
    share_v,
    slot_v,
    fields,
    statics,
    inverse,
    values,
    keys,
    owner_hot,
    spot_hot,
    sums_send,
    sums_recv,
    places,
    spots,
    land_sem,
    own_sem,
    halo_sem,
    a2a_send,
    a2a_recv,
):
    me = lax.axis_index("tile")
    cols, land_rows = precip.shape
    rows, width = head_init.shape
    full = rows + 2 * HALO
    chunks = width // LANES
    land_dev = land_rows // n
    per_chunk = LANES // (width // n)
    per_owner = slot_reach.shape[0] * LANES // n
    twins = LANES // per_owner
    reach_rows = reach_out.shape[0]
    tall = ((head_init, h), (subsurface_init, s), (conduct, g), (drain_rate, d), (flow_code, code))
    water, store, water2, store2 = (fields.at[i] for i in range(4))
    cond, sides, square, keep_h, keep_s, down_v, up_v, from_left, from_right = (
        statics.at[i] for i in range(9)
    )
    high_v, rest_v = values.at[0], values.at[1]
    owner_v, spot_v = keys.at[0], keys.at[1]

    land_copies = [
        pltpu.make_async_copy(ref, land_in.at[i], land_sem.at[i])
        for i, ref in enumerate((precip, pet, soil_init, ksat))
    ]
    land_copies.append(pltpu.make_async_copy(land_mask, mask_in, land_sem.at[4]))
    for copy in land_copies:
        copy.start()

    barrier = pltpu.get_barrier_semaphore()
    for k in range(1, n):
        pl.semaphore_signal(
            barrier, inc=1, device_id={"tile": lax.rem(me + k, n)}, device_id_type=MESH
        )

    own = [
        pltpu.make_async_copy(src, dst.at[pl.ds(HALO, rows)], own_sem.at[i])
        for i, (src, dst) in enumerate(tall)
    ]
    own.append(pltpu.make_async_copy(channel_share, share_v, own_sem.at[5]))
    own.append(pltpu.make_async_copy(cell_slot, slot_v, own_sem.at[6]))
    own.append(pltpu.make_async_copy(slot_reach.at[me // twins], places.at[me], own_sem.at[7]))
    for copy in own:
        copy.start()

    @pl.when(me == 0)
    def _():
        for _, dst in tall:
            dst[:HALO, :] = jnp.zeros((HALO, width), dst.dtype)

    @pl.when(me == n - 1)
    def _():
        for _, dst in tall:
            dst[full - HALO :, :] = jnp.zeros((HALO, width), dst.dtype)

    for copy in land_copies:
        copy.wait()
    rain, demand, moist, conductivity = land_in[0], land_in[1], land_in[2], land_in[3]
    mask = mask_in[...].astype(jnp.float32)
    wet = 2.0 * moist
    cap = conductivity * (1.0 - wet)
    runoff = mask * rain * rain / (rain + cap)
    drainage = 0.25 * mask * conductivity * (wet * wet) * (wet * wet)
    evap = mask * demand * wet
    soil_out[...] = moist + 0.1 * (mask * rain - runoff - drainage - evap)
    lane = lax.broadcasted_iota(jnp.int32, (cols, land_rows), 1)
    place = lax.rem(lane, land_dev)
    side = HALO // 4
    if 4 * cols < LANES:
        pack[4 * cols :, :] = jnp.zeros((LANES - 4 * cols, land_rows), jnp.float32)
    for i, x in enumerate((runoff, drainage)):
        pack[i * cols : (i + 1) * cols, :] = x
        before = jnp.where(lane >= land_dev, pltpu.roll(x, side, 1), 0.0)
        after = jnp.where(
            lane < land_rows - land_dev, pltpu.roll(x, land_rows - (land_dev - side), 1), 0.0
        )
        pack[(2 + i) * cols : (3 + i) * cols, :] = jnp.where(place < side, before, after)
    land_send[...] = jnp.transpose(pack[...]).reshape(n, land_dev, LANES)

    def drain(ref, sem):
        pltpu.make_async_copy(ref, ref, sem).wait()

    def to_peers(stage, source, target):
        for k in range(1, n):
            peer = lax.rem(me + k, n)
            pltpu.make_async_remote_copy(
                src_ref=source(peer),
                dst_ref=target,
                send_sem=a2a_send.at[stage],
                recv_sem=a2a_recv.at[stage],
                device_id={"tile": peer},
                device_id_type=MESH,
            ).start()

    pl.semaphore_wait(barrier, n - 1)
    own_land = land_recv.at[lax.rem(me, per_chunk), me // per_chunk]
    to_peers(0, lambda peer: land_send.at[peer], own_land)

    def halo_copy(i, up):
        src, dst = tall[i]
        if up:
            start, land, peer = (rows - ITERS, HALO - ITERS, me + 1)
        else:
            start, land, peer = (0, full - HALO, me - 1)
        return pltpu.make_async_remote_copy(
            src_ref=src.at[pl.ds(start, ITERS)],
            dst_ref=dst.at[pl.ds(land, ITERS)],
            send_sem=halo_sem.at[0 if up else 1],
            recv_sem=halo_sem.at[2 if up else 3],
            device_id={"tile": lax.rem(peer + n, n)},
            device_id_type=MESH,
        )

    @pl.when(me < n - 1)
    def _():
        for i in range(len(tall)):
            halo_copy(i, True).start()

    @pl.when(me > 0)
    def _():
        for i in range(len(tall)):
            halo_copy(i, False).start()

    to_peers(1, lambda peer: slot_reach.at[peer // twins], places.at[me])
    land_recv[lax.rem(me, per_chunk), me // per_chunk] = land_send[me]

    for copy in own:
        copy.wait()

    def at(c):
        return pl.ds(c * LANES, LANES)

    lane8 = lax.broadcasted_iota(jnp.int32, (TILE, LANES), 1)
    first = lane8 == 0
    last = lane8 == LANES - 1
    top8 = lax.broadcasted_iota(jnp.int32, (TILE, LANES), 0) < TILE // 2
    zero = jnp.zeros((TILE, LANES), jnp.float32)

    def rolled(x):
        return (pltpu.roll(x, 1, 1), pltpu.roll(x, LANES - 1, 1))

    def prepare(m):
        band = pl.ds(TILE * m, TILE)

        def load(c):
            gc, dc, kc = g[band, at(c)], d[band, at(c)], code[band, at(c)]
            down, up, right, left = (jnp.where(kc == q, dc, 0.0) for q in range(4))
            cond[c, band, :] = gc
            square[c, band, :] = gc * gc
            keep_s[c, band, :] = 1.0 - (down + up + right + left)
            down_v[c, band, :] = down
            up_v[c, band, :] = up
            return rolled(gc) + (pltpu.roll(right, 1, 1), pltpu.roll(left, LANES - 1, 1))

        before, here = (zero,) * 4, load(0)
        for c in range(chunks):
            after = load(c + 1) if c + 1 < chunks else (zero,) * 4
            sides[c, band, :] = jnp.where(first, before[0], here[0]) + jnp.where(last, after[1], here[1])
            from_left[c, band, :] = jnp.where(first, before[2], here[2])
            from_right[c, band, :] = jnp.where(last, after[3], here[3])
            before, here = here, after

    def finish(start):
        band, above, below = (pl.ds(start + q, TILE) for q in (0, -1, 1))
        for c in range(chunks):
            around = (cond[c, above, :] + cond[c, below, :]) + sides[c, band, :]
            keep_h[c, band, :] = 1.0 - cond[c, band, :] * around

    inner = range(1, 1 + rows // TILE)
    for m in inner:
        prepare(m)
        band, own_band = pl.ds(TILE * m, TILE), pl.ds(TILE * (m - 1), TILE)
        for c in range(chunks):
            inverse[c, own_band, :] = 1.0 / g[band, at(c)]
            slot = slot_v[own_band, at(c)]
            owner = slot // per_owner
            owner_v[c, own_band, :] = owner.astype(jnp.float32)
            spot_v[c, own_band, :] = (slot - owner * per_owner).astype(jnp.float32)
    for m in inner[1:-1]:
        finish(TILE * m)

    line = lax.broadcasted_iota(jnp.int32, (16, LANES), 0).astype(jnp.float32)
    lines = [(line + 16 * q).astype(jnp.bfloat16) for q in range(max(n, per_owner) // 16)]
    one, none = jnp.ones((16, LANES), jnp.bfloat16), jnp.zeros((16, LANES), jnp.bfloat16)

    def row_of(ref, c, r):
        half = ref[c, pl.ds(r, TILE, stride=0), :]
        return jnp.concatenate([half, half], axis=0).astype(jnp.bfloat16)

    def make_hot(r, carry):
        for c in range(chunks):
            for ref, hot, count in ((owner_v, owner_hot, n), (spot_v, spot_hot, per_owner)):
                key = row_of(ref, c, r)
                for q in range(count // 16):
                    hot[r, 16 * q : 16 * (q + 1), at(c)] = jnp.where(key == lines[q], one, none)
        return carry

    lax.fori_loop(0, rows, make_hot, 0, unroll=2)

    drain(land_send.at[pl.ds(0, n - 1)], a2a_send.at[0])
    drain(land_send.at[pl.ds(0, n - 1)], a2a_recv.at[0])

    l_iota = lax.broadcasted_iota(jnp.int32, (LANES, 4 * LANES), 0)
    f_iota = lax.broadcasted_iota(jnp.int32, (LANES, 4 * LANES), 1)
    cell = lax.rem(f_iota, LANES) // 4
    group = f_iota // LANES
    total = None
    for k in range(per_chunk):
        inside = (cell >= k * cols) & (cell < (k + 1) * cols)
        spread = inside & (l_iota == group * cols + cell - k * cols)
        spread = jnp.where(spread, 1.0, 0.0).astype(jnp.bfloat16)
        block = land_recv[k].reshape(chunks * land_dev, LANES)
        for part in parts_of(block, 3):
            term = jnp.dot(part, spread, preferred_element_type=jnp.float32)
            total = term if total is None else total + term
    wide[...] = total

    def fill(m):
        band = pl.ds(TILE * m, TILE)
        for c in range(chunks):
            added = []
            for i in range(2):
                pair = []
                for q in (2 * m, 2 * m + 1):
                    if q < side:
                        lanes, r = (2 + i) * LANES, q
                    elif q < side + land_dev:
                        lanes, r = i * LANES, q - side
                    else:
                        lanes, r = (2 + i) * LANES, q - land_dev
                    r = c * land_dev + r
                    pair.append(jnp.broadcast_to(wide[r : r + 1, lanes : lanes + LANES], (TILE, LANES)))
                added.append(jnp.where(top8, pair[0], pair[1]))
            water[c, band, :] = g[band, at(c)] * (h[band, at(c)] + added[0])
            store[c, band, :] = s[band, at(c)] + added[1]

    for m in inner:
        fill(m)

    halo_bytes = water.at[:, pl.ds(0, len(tall) * ITERS), :]

    @pl.when(me > 0)
    def _():
        drain(halo_bytes, halo_sem.at[2])

    @pl.when(me < n - 1)
    def _():
        drain(halo_bytes, halo_sem.at[3])

    outer = (0, full // TILE - 1)
    for m in outer:
        prepare(m)
        fill(m)
    for start in (1, HALO, full - 2 * HALO, full - HALO):
        finish(start)

    def advance(source, start, put):
        w, t = source

        def load(c):
            wc, tc = w[c, pl.ds(start, TILE), :], t[c, pl.ds(start, TILE), :]
            return (wc, tc) + rolled(wc) + rolled(tc)

        band, above, below = (pl.ds(start + q, TILE) for q in (0, -1, 1))
        before, here = (zero,) * 6, load(0)
        for c in range(chunks):
            after = load(c + 1) if c + 1 < chunks else (zero,) * 6
            flux = jnp.where(first, before[2], here[2]) + jnp.where(last, after[3], here[3])
            flux = flux + (w[c, above, :] + w[c, below, :])
            new_w = keep_h[c, band, :] * here[0] + square[c, band, :] * flux
            moved = from_left[c, band, :] * jnp.where(first, before[4], here[4])
            moved = moved + from_right[c, band, :] * jnp.where(last, after[5], here[5])
            moved = moved + (down_v[c, above, :] * t[c, above, :] + up_v[c, below, :] * t[c, below, :])
            put(c, new_w, keep_s[c, band, :] * here[1] + moved)
            before, here = here, after

    def substep(source, target, reach):
        for start in range(HALO - reach, HALO + rows + reach, TILE):

            def put(c, new_w, new_s):
                target[0][c, pl.ds(start, TILE), :] = new_w
                target[1][c, pl.ds(start, TILE), :] = new_s

            advance(source, start, put)

    one_side, other_side = (water, store), (water2, store2)
    substep(one_side, other_side, ITERS - 1)

    def two(_, carry):
        substep(other_side, one_side, ITERS - 2)
        substep(one_side, other_side, ITERS - 2)
        return carry

    lax.fori_loop(0, (ITERS - 2) // 2, two, 0)

    for start in range(HALO, HALO + rows, TILE):
        band = pl.ds(start - HALO, TILE)

        def put(c, new_w, new_s):
            depth = new_w * inverse[c, band, :]
            taken = share_v[band, at(c)] * depth
            head_out[band, at(c)] = depth - taken
            sub_out[band, at(c)] = new_s
            high = taken.astype(jnp.bfloat16).astype(jnp.float32)
            high_v[c, band, :] = high
            rest_v[c, band, :] = taken - high

        advance(other_side, start, put)

    def add_row(r, total):
        hot = owner_hot[r]
        left = []
        for ref in (high_v, rest_v):
            row = jnp.concatenate([row_of(ref, c, r) for c in range(chunks)], axis=1)
            left += [hot[16 * q : 16 * (q + 1)] * row for q in range(n // 16)]
        left = jnp.concatenate(left, axis=0)
        return total + lax.dot_general(left, spot_hot[r], NT, preferred_element_type=jnp.float32)

    total = lax.fori_loop(0, rows, add_row, jnp.zeros((2 * n, per_owner), jnp.float32), unroll=8)
    sums = total[:n] + total[n:]
    sums = jnp.concatenate([sums] * twins, axis=1)
    for k in range(n):
        sums_send[k] = sums[k : k + 1, :]
    sums_recv[me] = sums_send[me]
    to_peers(2, lambda peer: sums_send.at[peer], sums_recv.at[me])

    drain(places.at[pl.ds(0, n - 1)], a2a_send.at[1])
    drain(places.at[pl.ds(0, n - 1)], a2a_recv.at[1])
    half = lax.broadcasted_iota(jnp.int32, (1, LANES), 1) // per_owner == lax.rem(me, twins)
    lane_line = lax.broadcasted_iota(jnp.int32, (LANES, LANES), 0)
    reach_line = lax.broadcasted_iota(jnp.int32, (reach_rows, LANES), 0)
    for j in range(n):
        low = lax.rem(places[j], LANES)
        spots[:, at(j)] = jnp.where(half & (lane_line == low), 1.0, 0.0).astype(jnp.bfloat16)

    @pl.when(me < n - 1)
    def _():
        drain(halo_bytes, halo_sem.at[0])

    @pl.when(me > 0)
    def _():
        drain(halo_bytes, halo_sem.at[1])

    drain(sums_send.at[pl.ds(0, n - 1)], a2a_send.at[2])
    drain(sums_send.at[pl.ds(0, n - 1)], a2a_recv.at[2])
    found = []
    for j in range(n):
        high = places[j] // LANES
        found.append(jnp.where(reach_line == high, sums_recv[j], 0.0))
    found = jnp.concatenate(parts_of(jnp.concatenate(found, axis=1), 3), axis=0)
    reach = lax.dot_general(found, spots[...], NT, preferred_element_type=jnp.float32)
    reach_out[...] = reach[:reach_rows] + reach[reach_rows : 2 * reach_rows] + reach[2 * reach_rows :]


def flush(*refs):
    count = (len(refs) - 1) // 2
    copies = [
        pltpu.make_async_copy(src, dst, refs[-1].at[i])
        for i, (src, dst) in enumerate(zip(refs[:count], refs[count:-1]))
    ]
    for copy in copies:
        copy.start()
    for copy in copies:
        copy.wait()


def local(*args):
    n = lax.axis_size("tile")
    precip, head_init, slot_reach = args[0], args[5], args[12]
    cols, land_rows = precip.shape
    rows, width = head_init.shape
    slots = slot_reach.shape[0]
    full = rows + 2 * HALO
    land_dev = land_rows // n
    per_chunk = LANES // (width // n)
    chunks = width // LANES
    per_owner = slots // n
    f32, i32, b16 = jnp.float32, jnp.int32, jnp.bfloat16
    tall = pltpu.VMEM((full, width), f32)
    anywhere = pl.BlockSpec(memory_space=pl.ANY)
    soil, head, sub, reach = pl.pallas_call(
        functools.partial(kernel, n),
        out_shape=(
            pltpu.VMEM(precip.shape, f32),
            pltpu.VMEM(head_init.shape, f32),
            pltpu.VMEM(head_init.shape, f32),
            pltpu.VMEM((slots // LANES, LANES), f32),
        ),
        in_specs=[anywhere] * 13,
        out_specs=(pl.BlockSpec(memory_space=pltpu.VMEM),) * 4,
        scratch_shapes=[
            pltpu.VMEM((4, cols, land_rows), f32),
            pltpu.VMEM((cols, land_rows), i32),
            pltpu.VMEM((LANES, land_rows), f32),
            pltpu.VMEM((n, land_dev, LANES), f32),
            pltpu.VMEM((per_chunk, chunks, land_dev, LANES), f32),
            pltpu.VMEM((chunks * land_dev, 4 * LANES), f32),
            tall,
            tall,
            tall,
            tall,
            pltpu.VMEM((full, width), i32),
            pltpu.VMEM((rows, width), f32),
            pltpu.VMEM((rows, width), i32),
            pltpu.VMEM((4, chunks, full + TILE, LANES), f32),
            pltpu.VMEM((9, chunks, full + TILE, LANES), f32),
            pltpu.VMEM((chunks, rows, LANES), f32),
            pltpu.VMEM((2, chunks, rows + TILE, LANES), f32),
            pltpu.VMEM((2, chunks, rows + TILE, LANES), f32),
            pltpu.VMEM((rows, n, width), b16),
            pltpu.VMEM((rows, per_owner, width), b16),
            pltpu.VMEM((n, 1, LANES), f32),
            pltpu.VMEM((n, 1, LANES), f32),
            pltpu.VMEM((n, 1, LANES), i32),
            pltpu.VMEM((LANES, n * LANES), b16),
            pltpu.SemaphoreType.DMA((5,)),
            pltpu.SemaphoreType.DMA((8,)),
            pltpu.SemaphoreType.DMA((4,)),
            pltpu.SemaphoreType.DMA((3,)),
            pltpu.SemaphoreType.DMA((3,)),
        ],
        compiler_params=pltpu.CompilerParams(
            collective_id=0,
            has_side_effects=True,
            vmem_limit_bytes=40 * 2**20,
        ),
        name="step",
    )(*[pltpu.with_memory_space_constraint(x, pltpu.HBM) for x in (*args[:12], slot_reach.reshape(slots // LANES, 1, LANES))])
    results = (soil, head, sub, reach)
    soil, head, sub, reach = pl.pallas_call(
        flush,
        out_shape=tuple(jax.ShapeDtypeStruct(x.shape, x.dtype) for x in results),
        in_specs=[pl.BlockSpec(memory_space=pltpu.VMEM)] * 4,
        out_specs=(anywhere,) * 4,
        scratch_shapes=[pltpu.SemaphoreType.DMA((4,))],
        compiler_params=pltpu.CompilerParams(vmem_limit_bytes=2**20),
        name="flush",
    )(*results)
    return soil, head, sub, reach.reshape(slots)


def solution(mesh):
    grid = P(("member", "tile"), None)
    line = P(("member", "tile"))
    return jax.shard_map(
        local,
        mesh=mesh,
        in_specs=(grid,) * 12 + (line,),
        out_specs=(grid, grid, grid, line),
        check_vma=False,
    )
```

```python
import functools

import jax
import jax.numpy as jnp
from jax import lax
from jax.experimental import pallas as pl
from jax.experimental.pallas import tpu as pltpu
from jax.sharding import PartitionSpec as P

ITERS = 6
HALO = 8
TILE = 8
LANES = 128
MESH = pl.DeviceIdType.MESH
NT = (((1,), (1,)), ((), ()))


def parts_of(x, count):
    parts = []
    for _ in range(count):
        part = x.astype(jnp.bfloat16)
        parts.append(part)
        x = x - part.astype(jnp.float32)
    return parts


def kernel(
    n,
    precip,
    pet,
    soil_init,
    ksat,
    land_mask,
    head_init,
    subsurface_init,
    conduct,
    drain_rate,
    flow_code,
    channel_share,
    cell_slot,
    slot_reach,
    soil_out,
    head_out,
    sub_out,
    reach_out,
    land_in,
    mask_in,
    pack,
    land_send,
    land_recv,
    wide,
    h,
    s,
    g,
    d,
    code,
    share_v,
    slot_v,
    fields,
    statics,
    inverse,
    values,
    keys,
    owner_hot,
    spot_hot,
    sums_send,
    sums_recv,
    places,
    spots,
    middle,
    land_sem,
    own_sem,
    halo_sem,
    a2a_send,
    a2a_recv,
):
    me = lax.axis_index("tile")
    cols, land_rows = precip.shape
    rows, width = head_init.shape
    full = rows + 2 * HALO
    chunks = width // LANES
    land_dev = land_rows // n
    per_chunk = LANES // (width // n)
    per_owner = slot_reach.shape[0] * LANES // n
    twins = LANES // per_owner
    reach_rows = reach_out.shape[0]
    tall = ((head_init, h), (subsurface_init, s), (conduct, g), (drain_rate, d), (flow_code, code))
    states = [(fields.at[2 * i], fields.at[2 * i + 1]) for i in range(3)]
    water, store = states[0]
    half_way = ITERS // 2
    cond, sides, square, keep_h, keep_s, down_v, up_v, from_left, from_right = (
        statics.at[i] for i in range(9)
    )
    high_v, rest_v = values.at[0], values.at[1]
    owner_v, spot_v = keys.at[0], keys.at[1]

    land_copies = [
        pltpu.make_async_copy(ref, land_in.at[i], land_sem.at[i])
        for i, ref in enumerate((precip, pet, soil_init, ksat))
    ]
    land_copies.append(pltpu.make_async_copy(land_mask, mask_in, land_sem.at[4]))
    for copy in land_copies:
        copy.start()

    barrier = pltpu.get_barrier_semaphore()
    for k in range(1, n):
        pl.semaphore_signal(
            barrier, inc=1, device_id={"tile": lax.rem(me + k, n)}, device_id_type=MESH
        )

    own = [
        pltpu.make_async_copy(src, dst.at[pl.ds(HALO, rows)], own_sem.at[i])
        for i, (src, dst) in enumerate(tall)
    ]
    own.append(pltpu.make_async_copy(channel_share, share_v, own_sem.at[5]))
    own.append(pltpu.make_async_copy(cell_slot, slot_v, own_sem.at[6]))
    own.append(pltpu.make_async_copy(slot_reach.at[me // twins], places.at[me], own_sem.at[7]))
    for copy in own:
        copy.start()

    @pl.when(me == 0)
    def _():
        for _, dst in tall:
            dst[:HALO, :] = jnp.zeros((HALO, width), dst.dtype)
        middle[0] = jnp.zeros(middle.shape[1:], jnp.float32)

    @pl.when(me == n - 1)
    def _():
        for _, dst in tall:
            dst[full - HALO :, :] = jnp.zeros((HALO, width), dst.dtype)
        middle[1] = jnp.zeros(middle.shape[1:], jnp.float32)

    for copy in land_copies:
        copy.wait()
    rain, demand, moist, conductivity = land_in[0], land_in[1], land_in[2], land_in[3]
    mask = mask_in[...].astype(jnp.float32)
    wet = 2.0 * moist
    cap = conductivity * (1.0 - wet)
    runoff = mask * rain * rain / (rain + cap)
    drainage = 0.25 * mask * conductivity * (wet * wet) * (wet * wet)
    evap = mask * demand * wet
    soil_out[...] = moist + 0.1 * (mask * rain - runoff - drainage - evap)
    lane = lax.broadcasted_iota(jnp.int32, (cols, land_rows), 1)
    place = lax.rem(lane, land_dev)
    side = HALO // 4
    if 4 * cols < LANES:
        pack[4 * cols :, :] = jnp.zeros((LANES - 4 * cols, land_rows), jnp.float32)
    for i, x in enumerate((runoff, drainage)):
        pack[i * cols : (i + 1) * cols, :] = x
        before = jnp.where(lane >= land_dev, pltpu.roll(x, side, 1), 0.0)
        after = jnp.where(
            lane < land_rows - land_dev, pltpu.roll(x, land_rows - (land_dev - side), 1), 0.0
        )
        pack[(2 + i) * cols : (3 + i) * cols, :] = jnp.where(place < side, before, after)
    land_send[...] = jnp.transpose(pack[...]).reshape(n, land_dev, LANES)

    def drain(ref, sem):
        pltpu.make_async_copy(ref, ref, sem).wait()

    def to_peers(stage, source, target):
        for k in range(1, n):
            peer = lax.rem(me + k, n)
            pltpu.make_async_remote_copy(
                src_ref=source(peer),
                dst_ref=target,
                send_sem=a2a_send.at[stage],
                recv_sem=a2a_recv.at[stage],
                device_id={"tile": peer},
                device_id_type=MESH,
            ).start()

    def at(c):
        return pl.ds(c * LANES, LANES)

    lane8 = lax.broadcasted_iota(jnp.int32, (TILE, LANES), 1)
    first = lane8 == 0
    last = lane8 == LANES - 1
    top8 = lax.broadcasted_iota(jnp.int32, (TILE, LANES), 0) < TILE // 2
    zero = jnp.zeros((TILE, LANES), jnp.float32)

    def rolled(x):
        return (pltpu.roll(x, 1, 1), pltpu.roll(x, LANES - 1, 1))

    def prepare(m):
        band = pl.ds(TILE * m, TILE)

        def load(c):
            gc, dc, kc = g[band, at(c)], d[band, at(c)], code[band, at(c)]
            down, up, right, left = (jnp.where(kc == q, dc, 0.0) for q in range(4))
            cond[c, band, :] = gc
            square[c, band, :] = gc * gc
            keep_s[c, band, :] = 1.0 - (down + up + right + left)
            down_v[c, band, :] = down
            up_v[c, band, :] = up
            return rolled(gc) + (pltpu.roll(right, 1, 1), pltpu.roll(left, LANES - 1, 1))

        before, here = (zero,) * 4, load(0)
        for c in range(chunks):
            after = load(c + 1) if c + 1 < chunks else (zero,) * 4
            sides[c, band, :] = jnp.where(first, before[0], here[0]) + jnp.where(last, after[1], here[1])
            from_left[c, band, :] = jnp.where(first, before[2], here[2])
            from_right[c, band, :] = jnp.where(last, after[3], here[3])
            before, here = here, after

    def finish(start):
        band, above, below = (pl.ds(start + q, TILE) for q in (0, -1, 1))
        for c in range(chunks):
            around = (cond[c, above, :] + cond[c, below, :]) + sides[c, band, :]
            keep_h[c, band, :] = 1.0 - cond[c, band, :] * around

    line = lax.broadcasted_iota(jnp.int32, (16, LANES), 0).astype(jnp.float32)
    lines = [(line + 16 * q).astype(jnp.bfloat16) for q in range(max(n, per_owner) // 16)]
    one, none = jnp.ones((16, LANES), jnp.bfloat16), jnp.zeros((16, LANES), jnp.bfloat16)

    def row_of(ref, c, r):
        half = ref[c, pl.ds(r, TILE, stride=0), :]
        return jnp.concatenate([half, half], axis=0).astype(jnp.bfloat16)

    def make_hot(r, carry):
        for ref, hot, count in ((owner_v, owner_hot, n), (spot_v, spot_hot, per_owner)):
            for c in range(chunks):
                key = row_of(ref, c, r)
                for q in range(count // 16):
                    hot[r, 16 * q : 16 * (q + 1), at(c)] = jnp.where(key == lines[q], one, none)
        return carry

    inner = range(1, 1 + rows // TILE)

    def local_work():
        for copy in own:
            copy.wait()
        for m in inner:
            prepare(m)
            band, own_band = pl.ds(TILE * m, TILE), pl.ds(TILE * (m - 1), TILE)
            for c in range(chunks):
                inverse[c, own_band, :] = 1.0 / g[band, at(c)]
                slot = slot_v[own_band, at(c)]
                owner = slot // per_owner
                owner_v[c, own_band, :] = owner.astype(jnp.float32)
                spot_v[c, own_band, :] = (slot - owner * per_owner).astype(jnp.float32)
        for start in (*range(HALO + 1, HALO + rows - TILE, TILE), HALO + rows - TILE - 1):
            finish(start)
        lax.fori_loop(0, rows, make_hot, 0)

    @pl.when(me < n // 2)
    def _():
        local_work()

    pl.semaphore_wait(barrier, n - 1)
    own_land = land_recv.at[lax.rem(me, per_chunk), me // per_chunk]
    to_peers(0, lambda peer: land_send.at[peer], own_land)

    def halo_copy(i, up):
        src, dst = tall[i]
        if up:
            start, land, peer = (rows - half_way, HALO - half_way, me + 1)
        else:
            start, land, peer = (0, full - HALO, me - 1)
        return pltpu.make_async_remote_copy(
            src_ref=src.at[pl.ds(start, half_way)],
            dst_ref=dst.at[pl.ds(land, half_way)],
            send_sem=halo_sem.at[0 if up else 1],
            recv_sem=halo_sem.at[2 if up else 3],
            device_id={"tile": lax.rem(peer + n, n)},
            device_id_type=MESH,
        )

    @pl.when(me < n - 1)
    def _():
        for i in range(len(tall)):
            halo_copy(i, True).start()

    @pl.when(me > 0)
    def _():
        for i in range(len(tall)):
            halo_copy(i, False).start()

    to_peers(1, lambda peer: slot_reach.at[peer // twins], places.at[me])
    land_recv[lax.rem(me, per_chunk), me // per_chunk] = land_send[me]

    @pl.when(me >= n // 2)
    def _():
        local_work()

    halo_bytes = water.at[:, pl.ds(0, len(tall) * half_way), :]

    @pl.when(me > 0)
    def _():
        drain(halo_bytes, halo_sem.at[2])

    @pl.when(me < n - 1)
    def _():
        drain(halo_bytes, halo_sem.at[3])

    outer = (0, full // TILE - 1)
    for m in outer:
        prepare(m)
    for start in (1, HALO + rows - 1):
        finish(start)

    drain(land_send.at[pl.ds(0, n - 1)], a2a_send.at[0])
    drain(land_send.at[pl.ds(0, n - 1)], a2a_recv.at[0])

    l_iota = lax.broadcasted_iota(jnp.int32, (LANES, 4 * LANES), 0)
    f_iota = lax.broadcasted_iota(jnp.int32, (LANES, 4 * LANES), 1)
    cell = lax.rem(f_iota, LANES) // 4
    group = f_iota // LANES
    total = None
    for k in range(per_chunk):
        inside = (cell >= k * cols) & (cell < (k + 1) * cols)
        spread = inside & (l_iota == group * cols + cell - k * cols)
        spread = jnp.where(spread, 1.0, 0.0).astype(jnp.bfloat16)
        block = land_recv[k].reshape(chunks * land_dev, LANES)
        for part in parts_of(block, 3):
            term = jnp.dot(part, spread, preferred_element_type=jnp.float32)
            total = term if total is None else total + term
    wide[...] = total

    def fill(m):
        band = pl.ds(TILE * m, TILE)
        for c in range(chunks):
            added = []
            for i in range(2):
                pair = []
                for q in (2 * m, 2 * m + 1):
                    if q < side:
                        lanes, r = (2 + i) * LANES, q
                    elif q < side + land_dev:
                        lanes, r = i * LANES, q - side
                    else:
                        lanes, r = (2 + i) * LANES, q - land_dev
                    r = c * land_dev + r
                    pair.append(jnp.broadcast_to(wide[r : r + 1, lanes : lanes + LANES], (TILE, LANES)))
                added.append(jnp.where(top8, pair[0], pair[1]))
            water[c, band, :] = g[band, at(c)] * (h[band, at(c)] + added[0])
            store[c, band, :] = s[band, at(c)] + added[1]

    for m in (*outer, *inner):
        fill(m)

    def advance(source, start, put):
        w, t = source

        def load(c):
            wc, tc = w[c, pl.ds(start, TILE), :], t[c, pl.ds(start, TILE), :]
            return (wc, tc) + rolled(wc) + rolled(tc)

        band, above, below = (pl.ds(start + q, TILE) for q in (0, -1, 1))
        before, here = (zero,) * 6, load(0)
        for c in range(chunks):
            after = load(c + 1) if c + 1 < chunks else (zero,) * 6
            flux = jnp.where(first, before[2], here[2]) + jnp.where(last, after[3], here[3])
            flux = flux + (w[c, above, :] + w[c, below, :])
            new_w = keep_h[c, band, :] * here[0] + square[c, band, :] * flux
            moved = from_left[c, band, :] * jnp.where(first, before[4], here[4])
            moved = moved + from_right[c, band, :] * jnp.where(last, after[5], here[5])
            moved = moved + (down_v[c, above, :] * t[c, above, :] + up_v[c, below, :] * t[c, below, :])
            put(c, new_w, keep_s[c, band, :] * here[1] + moved)
            before, here = here, after

    def substep(source, target, starts):
        for start in starts:

            def put(c, new_w, new_s):
                target[0][c, pl.ds(start, TILE), :] = new_w
                target[1][c, pl.ds(start, TILE), :] = new_s

            advance(source, start, put)

    def last_step(source, starts):
        for start in starts:
            band = pl.ds(start - HALO, TILE)

            def put(c, new_w, new_s):
                depth = new_w * inverse[c, band, :]
                taken = share_v[band, at(c)] * depth
                head_out[band, at(c)] = depth - taken
                sub_out[band, at(c)] = new_s
                high = taken.astype(jnp.bfloat16).astype(jnp.float32)
                high_v[c, band, :] = high
                rest_v[c, band, :] = taken - high

            advance(source, start, put)

    top, end = HALO, HALO + rows
    state, target = 0, 1
    for reach in range(half_way - 1, 0, -1):
        substep(states[state], states[target], range(top - reach, end + reach, TILE))
        state, target = target, state
    substep(states[state], states[target], (top, end - TILE))

    def middle_copy(down):
        start = end - half_way if down else top
        return pltpu.make_async_remote_copy(
            src_ref=fields.at[pl.ds(2 * target, 2), :, pl.ds(start, half_way), :],
            dst_ref=middle.at[0 if down else 1],
            send_sem=halo_sem.at[4 if down else 5],
            recv_sem=halo_sem.at[6 if down else 7],
            device_id={"tile": lax.rem(me + (1 if down else n - 1), n)},
            device_id_type=MESH,
        )

    @pl.when(me < n - 1)
    def _():
        middle_copy(True).start()

    @pl.when(me > 0)
    def _():
        middle_copy(False).start()

    substep(states[state], states[target], range(top + TILE, end - TILE, TILE))
    path = (target, state, 2)
    later = ITERS - half_way - 1
    for q in range(later):
        low = top + TILE - (later - q)
        substep(states[path[q]], states[path[q + 1]], range(low, end - TILE + (later - q), TILE))
    last_step(states[path[later]], range(top + TILE, end - TILE, TILE))

    def add_row(r, total):
        hot = owner_hot[r]
        left = []
        for ref in (high_v, rest_v):
            row = jnp.concatenate([row_of(ref, c, r) for c in range(chunks)], axis=1)
            left += [hot[16 * q : 16 * (q + 1)] * row for q in range(n // 16)]
        left = jnp.concatenate(left, axis=0)
        return total + lax.dot_general(left, spot_hot[r], NT, preferred_element_type=jnp.float32)

    total = jnp.zeros((2 * n, per_owner), jnp.float32)
    total = lax.fori_loop(TILE, rows - TILE, add_row, total, unroll=8)

    @pl.when(me > 0)
    def _():
        middle_copy(True).wait_recv()

    @pl.when(me < n - 1)
    def _():
        middle_copy(False).wait_recv()

    for i in range(2):
        for c in range(chunks):
            fields[2 * path[0] + i, c, top - half_way : top, :] = middle[0, i, c]
            fields[2 * path[0] + i, c, end : end + half_way, :] = middle[1, i, c]
    for q in range(later):
        reach = later - q
        substep(states[path[q]], states[path[q + 1]], (top - reach, end - TILE + reach))
    last_step(states[path[later]], (top, end - TILE))
    total = lax.fori_loop(0, TILE, add_row, total, unroll=8)
    total = lax.fori_loop(rows - TILE, rows, add_row, total, unroll=8)
    sums = total[:n] + total[n:]
    sums = jnp.concatenate([sums] * twins, axis=1)
    for k in range(n):
        sums_send[k] = sums[k : k + 1, :]
    sums_recv[me] = sums_send[me]
    to_peers(2, lambda peer: sums_send.at[peer], sums_recv.at[me])

    drain(places.at[pl.ds(0, n - 1)], a2a_send.at[1])
    drain(places.at[pl.ds(0, n - 1)], a2a_recv.at[1])
    half = lax.broadcasted_iota(jnp.int32, (1, LANES), 1) // per_owner == lax.rem(me, twins)
    lane_line = lax.broadcasted_iota(jnp.int32, (LANES, LANES), 0)
    reach_line = lax.broadcasted_iota(jnp.int32, (reach_rows, LANES), 0)
    for j in range(n):
        low = lax.rem(places[j], LANES)
        spots[:, at(j)] = jnp.where(half & (lane_line == low), 1.0, 0.0).astype(jnp.bfloat16)

    @pl.when(me < n - 1)
    def _():
        drain(halo_bytes, halo_sem.at[0])
        middle_copy(True).wait_send()

    @pl.when(me > 0)
    def _():
        drain(halo_bytes, halo_sem.at[1])
        middle_copy(False).wait_send()

    drain(sums_send.at[pl.ds(0, n - 1)], a2a_send.at[2])
    drain(sums_send.at[pl.ds(0, n - 1)], a2a_recv.at[2])
    found = []
    for j in range(n):
        high = places[j] // LANES
        found.append(jnp.where(reach_line == high, sums_recv[j], 0.0))
    found = jnp.concatenate(parts_of(jnp.concatenate(found, axis=1), 3), axis=0)
    reach = lax.dot_general(found, spots[...], NT, preferred_element_type=jnp.float32)
    reach_out[...] = reach[:reach_rows] + reach[reach_rows : 2 * reach_rows] + reach[2 * reach_rows :]


def flush(*refs):
    count = (len(refs) - 1) // 2
    copies = [
        pltpu.make_async_copy(src, dst, refs[-1].at[i])
        for i, (src, dst) in enumerate(zip(refs[:count], refs[count:-1]))
    ]
    for copy in copies:
        copy.start()
    for copy in copies:
        copy.wait()


def local(*args):
    n = lax.axis_size("tile")
    precip, head_init, slot_reach = args[0], args[5], args[12]
    cols, land_rows = precip.shape
    rows, width = head_init.shape
    slots = slot_reach.shape[0]
    full = rows + 2 * HALO
    land_dev = land_rows // n
    per_chunk = LANES // (width // n)
    chunks = width // LANES
    per_owner = slots // n
    f32, i32, b16 = jnp.float32, jnp.int32, jnp.bfloat16
    tall = pltpu.VMEM((full, width), f32)
    anywhere = pl.BlockSpec(memory_space=pl.ANY)
    soil, head, sub, reach = pl.pallas_call(
        functools.partial(kernel, n),
        out_shape=(
            pltpu.VMEM(precip.shape, f32),
            pltpu.VMEM(head_init.shape, f32),
            pltpu.VMEM(head_init.shape, f32),
            pltpu.VMEM((slots // LANES, LANES), f32),
        ),
        in_specs=[anywhere] * 13,
        out_specs=(pl.BlockSpec(memory_space=pltpu.VMEM),) * 4,
        scratch_shapes=[
            pltpu.VMEM((4, cols, land_rows), f32),
            pltpu.VMEM((cols, land_rows), i32),
            pltpu.VMEM((LANES, land_rows), f32),
            pltpu.VMEM((n, land_dev, LANES), f32),
            pltpu.VMEM((per_chunk, chunks, land_dev, LANES), f32),
            pltpu.VMEM((chunks * land_dev, 4 * LANES), f32),
            tall,
            tall,
            tall,
            tall,
            pltpu.VMEM((full, width), i32),
            pltpu.VMEM((rows, width), f32),
            pltpu.VMEM((rows, width), i32),
            pltpu.VMEM((6, chunks, full + TILE, LANES), f32),
            pltpu.VMEM((9, chunks, full + TILE, LANES), f32),
            pltpu.VMEM((chunks, rows, LANES), f32),
            pltpu.VMEM((2, chunks, rows + TILE, LANES), f32),
            pltpu.VMEM((2, chunks, rows + TILE, LANES), f32),
            pltpu.VMEM((rows, n, width), b16),
            pltpu.VMEM((rows, per_owner, width), b16),
            pltpu.VMEM((n, 1, LANES), f32),
            pltpu.VMEM((n, 1, LANES), f32),
            pltpu.VMEM((n, 1, LANES), i32),
            pltpu.VMEM((LANES, n * LANES), b16),
            pltpu.VMEM((2, 2, chunks, ITERS // 2, LANES), f32),
            pltpu.SemaphoreType.DMA((5,)),
            pltpu.SemaphoreType.DMA((8,)),
            pltpu.SemaphoreType.DMA((8,)),
            pltpu.SemaphoreType.DMA((3,)),
            pltpu.SemaphoreType.DMA((3,)),
        ],
        compiler_params=pltpu.CompilerParams(
            collective_id=0,
            has_side_effects=True,
            vmem_limit_bytes=40 * 2**20,
        ),
        name="step",
    )(*[pltpu.with_memory_space_constraint(x, pltpu.HBM) for x in (*args[:12], slot_reach.reshape(slots // LANES, 1, LANES))])
    results = (soil, head, sub, reach)
    soil, head, sub, reach = pl.pallas_call(
        flush,
        out_shape=tuple(jax.ShapeDtypeStruct(x.shape, x.dtype) for x in results),
        in_specs=[pl.BlockSpec(memory_space=pltpu.VMEM)] * 4,
        out_specs=(anywhere,) * 4,
        scratch_shapes=[pltpu.SemaphoreType.DMA((4,))],
        compiler_params=pltpu.CompilerParams(vmem_limit_bytes=2**20),
        name="flush",
    )(*results)
    return soil, head, sub, reach.reshape(slots)


def solution(mesh):
    grid = P(("member", "tile"), None)
    line = P(("member", "tile"))
    return jax.shard_map(
        local,
        mesh=mesh,
        in_specs=(grid,) * 12 + (line,),
        out_specs=(grid, grid, grid, line),
        check_vma=False,
    )
```

```python
import functools

import jax
import jax.numpy as jnp
from jax import lax
from jax.experimental import pallas as pl
from jax.experimental.pallas import tpu as pltpu
from jax.sharding import PartitionSpec as P

ITERS = 6
HALO = 8
TILE = 8
LANES = 128
MESH = pl.DeviceIdType.MESH
NT = (((1,), (1,)), ((), ()))


def parts_of(x, count):
    parts = []
    for _ in range(count):
        part = x.astype(jnp.bfloat16)
        parts.append(part)
        x = x - part.astype(jnp.float32)
    return parts


def kernel(
    n,
    precip,
    pet,
    soil_init,
    ksat,
    land_mask,
    head_init,
    subsurface_init,
    conduct,
    drain_rate,
    flow_code,
    channel_share,
    cell_slot,
    slot_reach,
    soil_out,
    head_out,
    sub_out,
    reach_out,
    land_in,
    mask_in,
    pack,
    land_send,
    land_recv,
    wide,
    h,
    s,
    g,
    d,
    code,
    share_v,
    slot_v,
    fields,
    statics,
    inverse,
    ratio,
    final,
    values,
    keys,
    owner_hot,
    spot_hot,
    sums_send,
    sums_recv,
    places,
    spots,
    middle,
    land_sem,
    own_sem,
    halo_sem,
    a2a_send,
    a2a_recv,
):
    me = lax.axis_index("tile")
    cols, land_rows = precip.shape
    rows, width = head_init.shape
    full = rows + 2 * HALO
    chunks = width // LANES
    land_dev = land_rows // n
    per_chunk = LANES // (width // n)
    per_owner = slot_reach.shape[0] * LANES // n
    twins = LANES // per_owner
    reach_rows = reach_out.shape[0]
    tall = ((head_init, h), (subsurface_init, s), (conduct, g), (drain_rate, d), (flow_code, code))
    states = [fields.at[i] for i in range(6)]
    water, store = states[0], states[3]
    half_way = ITERS // 2
    cond, sides, square, keep_h, keep_s, down_v, up_v, from_left, from_right = (
        statics.at[i] for i in range(9)
    )
    high_v, rest_v = values.at[0], values.at[1]
    owner_v, spot_v = keys.at[0], keys.at[1]

    land_copies = [
        pltpu.make_async_copy(ref, land_in.at[i], land_sem.at[0])
        for i, ref in enumerate((precip, pet, soil_init, ksat))
    ]
    land_copies.append(pltpu.make_async_copy(land_mask, mask_in, land_sem.at[1]))
    for copy in land_copies:
        copy.start()

    barrier = pltpu.get_barrier_semaphore()
    for k in range(1, n):
        pl.semaphore_signal(
            barrier, inc=1, device_id={"tile": lax.rem(me + k, n)}, device_id_type=MESH
        )

    own = [
        pltpu.make_async_copy(src, dst.at[pl.ds(HALO, rows)], own_sem.at[i])
        for i, (src, dst) in enumerate(tall)
    ]
    own.append(pltpu.make_async_copy(channel_share, share_v, own_sem.at[5]))
    own.append(pltpu.make_async_copy(cell_slot, slot_v, own_sem.at[6]))
    own.append(pltpu.make_async_copy(slot_reach.at[me // twins], places.at[me], own_sem.at[7]))
    for copy in own:
        copy.start()

    @pl.when(me == 0)
    def _():
        for _, dst in tall:
            dst[:HALO, :] = jnp.zeros((HALO, width), dst.dtype)
        middle[0] = jnp.zeros(middle.shape[1:], jnp.float32)

    @pl.when(me == n - 1)
    def _():
        for _, dst in tall:
            dst[full - HALO :, :] = jnp.zeros((HALO, width), dst.dtype)
        middle[1] = jnp.zeros(middle.shape[1:], jnp.float32)

    land_copies[-1].wait()
    pltpu.make_async_copy(land_in, land_in, land_sem.at[0]).wait()
    rain, demand, moist, conductivity = land_in[0], land_in[1], land_in[2], land_in[3]
    mask = mask_in[...].astype(jnp.float32)
    wet = 2.0 * moist
    cap = conductivity * (1.0 - wet)
    runoff = mask * rain * rain / (rain + cap)
    drainage = 0.25 * mask * conductivity * (wet * wet) * (wet * wet)
    evap = mask * demand * wet
    soil_out[...] = moist + 0.1 * (mask * rain - runoff - drainage - evap)
    lane = lax.broadcasted_iota(jnp.int32, (cols, land_rows), 1)
    place = lax.rem(lane, land_dev)
    side = HALO // 4
    if 4 * cols < LANES:
        pack[4 * cols :, :] = jnp.zeros((LANES - 4 * cols, land_rows), jnp.float32)
    for i, x in enumerate((runoff, drainage)):
        pack[i * cols : (i + 1) * cols, :] = x
        before = jnp.where(lane >= land_dev, pltpu.roll(x, side, 1), 0.0)
        after = jnp.where(
            lane < land_rows - land_dev, pltpu.roll(x, land_rows - (land_dev - side), 1), 0.0
        )
        pack[(2 + i) * cols : (3 + i) * cols, :] = jnp.where(place < side, before, after)
    land_send[...] = jnp.transpose(pack[...]).reshape(n, land_dev, LANES)

    def drain(ref, sem):
        pltpu.make_async_copy(ref, ref, sem).wait()

    def to_peers(stage, source, target):
        for k in range(1, n):
            peer = lax.rem(me + jnp.where(me < n // 2, n - k, k), n)
            pltpu.make_async_remote_copy(
                src_ref=source(peer),
                dst_ref=target,
                send_sem=a2a_send.at[stage],
                recv_sem=a2a_recv.at[stage],
                device_id={"tile": peer},
                device_id_type=MESH,
            ).start()

    def at(c):
        return pl.ds(c * LANES, LANES)

    lane8 = lax.broadcasted_iota(jnp.int32, (TILE, LANES), 1)
    first = lane8 == 0
    last = lane8 == LANES - 1
    top8 = lax.broadcasted_iota(jnp.int32, (TILE, LANES), 0) < TILE // 2
    zero = jnp.zeros((TILE, LANES), jnp.float32)

    def rolled(x):
        return (pltpu.roll(x, 1, 1), pltpu.roll(x, LANES - 1, 1))

    def prepare(m):
        band = pl.ds(TILE * m, TILE)

        def load(c):
            gc, dc, kc = g[band, at(c)], d[band, at(c)], code[band, at(c)]
            down, up, right, left = (jnp.where(kc == q, dc, 0.0) for q in range(4))
            cond[c, band, :] = gc
            square[c, band, :] = gc * gc
            keep_s[c, band, :] = 1.0 - (down + up + right + left)
            down_v[c, band, :] = down
            up_v[c, band, :] = up
            return rolled(gc) + (pltpu.roll(right, 1, 1), pltpu.roll(left, LANES - 1, 1))

        before, here = (zero,) * 4, load(0)
        for c in range(chunks):
            after = load(c + 1) if c + 1 < chunks else (zero,) * 4
            sides[c, band, :] = jnp.where(first, before[0], here[0]) + jnp.where(last, after[1], here[1])
            from_left[c, band, :] = jnp.where(first, before[2], here[2])
            from_right[c, band, :] = jnp.where(last, after[3], here[3])
            before, here = here, after

    def finish(start):
        band, above, below = (pl.ds(start + q, TILE) for q in (0, -1, 1))
        for c in range(chunks):
            around = (cond[c, above, :] + cond[c, below, :]) + sides[c, band, :]
            keep_h[c, band, :] = 1.0 - cond[c, band, :] * around

    line = lax.broadcasted_iota(jnp.int32, (16, LANES), 0).astype(jnp.float32)
    lines = [(line + 16 * q).astype(jnp.bfloat16) for q in range(max(n, per_owner) // 16)]
    one, none = jnp.ones((16, LANES), jnp.bfloat16), jnp.zeros((16, LANES), jnp.bfloat16)

    def row_of(ref, c, r):
        half = ref[c, pl.ds(r, TILE, stride=0), :]
        return jnp.concatenate([half, half], axis=0).astype(jnp.bfloat16)

    def make_hot(r, carry):
        for ref, hot, count in ((owner_v, owner_hot, n), (spot_v, spot_hot, per_owner)):
            for c in range(chunks):
                key = row_of(ref, c, r)
                for q in range(count // 16):
                    hot[r, 16 * q : 16 * (q + 1), at(c)] = jnp.where(key == lines[q], one, none)
        return carry

    inner = range(1, 1 + rows // TILE)

    def local_work():
        for copy in own:
            copy.wait()
        for m in inner:
            prepare(m)
            band, own_band = pl.ds(TILE * m, TILE), pl.ds(TILE * (m - 1), TILE)
            for c in range(chunks):
                backward = 1.0 / g[band, at(c)]
                inverse[c, own_band, :] = backward
                ratio[c, own_band, :] = share_v[own_band, at(c)] * backward
                slot = slot_v[own_band, at(c)]
                owner = slot // per_owner
                owner_v[c, own_band, :] = owner.astype(jnp.float32)
                spot_v[c, own_band, :] = (slot - owner * per_owner).astype(jnp.float32)
        for start in (*range(HALO + 1, HALO + rows - TILE, TILE), HALO + rows - TILE - 1):
            finish(start)
        lax.fori_loop(0, rows, make_hot, 0)

    @pl.when(me < n // 2)
    def _():
        local_work()

    pl.semaphore_wait(barrier, n - 1)
    own_land = land_recv.at[lax.rem(me, per_chunk), me // per_chunk]
    to_peers(0, lambda peer: land_send.at[peer], own_land)

    def halo_copy(i, up):
        src, dst = tall[i]
        if up:
            start, land, peer = (rows - half_way, HALO - half_way, me + 1)
        else:
            start, land, peer = (0, full - HALO, me - 1)
        return pltpu.make_async_remote_copy(
            src_ref=src.at[pl.ds(start, half_way)],
            dst_ref=dst.at[pl.ds(land, half_way)],
            send_sem=halo_sem.at[0 if up else 1],
            recv_sem=halo_sem.at[2 if up else 3],
            device_id={"tile": lax.rem(peer + n, n)},
            device_id_type=MESH,
        )

    @pl.when(me < n - 1)
    def _():
        for i in range(len(tall)):
            halo_copy(i, True).start()

    @pl.when(me > 0)
    def _():
        for i in range(len(tall)):
            halo_copy(i, False).start()

    to_peers(1, lambda peer: slot_reach.at[peer // twins], places.at[me])
    land_recv[lax.rem(me, per_chunk), me // per_chunk] = land_send[me]

    @pl.when(me >= n // 2)
    def _():
        local_work()

    halo_bytes = water.at[:, pl.ds(0, len(tall) * half_way), :]

    @pl.when(me > 0)
    def _():
        drain(halo_bytes, halo_sem.at[2])

    @pl.when(me < n - 1)
    def _():
        drain(halo_bytes, halo_sem.at[3])

    outer = (0, full // TILE - 1)
    for m in outer:
        prepare(m)
    for start in (1, HALO + rows - 1):
        finish(start)

    drain(land_send.at[pl.ds(0, n - 1)], a2a_send.at[0])
    drain(land_send.at[pl.ds(0, n - 1)], a2a_recv.at[0])

    l_iota = lax.broadcasted_iota(jnp.int32, (LANES, 4 * LANES), 0)
    f_iota = lax.broadcasted_iota(jnp.int32, (LANES, 4 * LANES), 1)
    cell = lax.rem(f_iota, LANES) // 4
    group = f_iota // LANES
    total = None
    for k in range(per_chunk):
        inside = (cell >= k * cols) & (cell < (k + 1) * cols)
        spread = inside & (l_iota == group * cols + cell - k * cols)
        spread = jnp.where(spread, 1.0, 0.0).astype(jnp.bfloat16)
        block = land_recv[k].reshape(chunks * land_dev, LANES)
        for part in parts_of(block, 3):
            term = jnp.dot(part, spread, preferred_element_type=jnp.float32)
            total = term if total is None else total + term
    wide[...] = total

    def fill(m, i):
        band = pl.ds(TILE * m, TILE)
        for c in range(chunks):
            pair = []
            for q in (2 * m, 2 * m + 1):
                if q < side:
                    lanes, r = (2 + i) * LANES, q
                elif q < side + land_dev:
                    lanes, r = i * LANES, q - side
                else:
                    lanes, r = (2 + i) * LANES, q - land_dev
                r = c * land_dev + r
                pair.append(jnp.broadcast_to(wide[r : r + 1, lanes : lanes + LANES], (TILE, LANES)))
            added = jnp.where(top8, pair[0], pair[1])
            if i == 0:
                water[c, band, :] = g[band, at(c)] * (h[band, at(c)] + added)
            else:
                store[c, band, :] = s[band, at(c)] + added

    for m in (*outer, *inner):
        fill(m, 0)

    def advance_water(w, start, put):
        def load(c):
            wc = w[c, pl.ds(start, TILE), :]
            return (wc,) + rolled(wc)

        band, above, below = (pl.ds(start + q, TILE) for q in (0, -1, 1))
        before, here = (zero,) * 3, load(0)
        for c in range(chunks):
            after = load(c + 1) if c + 1 < chunks else (zero,) * 3
            flux = jnp.where(first, before[1], here[1]) + jnp.where(last, after[2], here[2])
            flux = flux + (w[c, above, :] + w[c, below, :])
            put(c, keep_h[c, band, :] * here[0] + square[c, band, :] * flux)
            before, here = here, after

    def advance_store(t, start, put):
        def load(c):
            tc = t[c, pl.ds(start, TILE), :]
            return (tc,) + rolled(tc)

        band, above, below = (pl.ds(start + q, TILE) for q in (0, -1, 1))
        before, here = (zero,) * 3, load(0)
        for c in range(chunks):
            after = load(c + 1) if c + 1 < chunks else (zero,) * 3
            moved = from_left[c, band, :] * jnp.where(first, before[1], here[1])
            moved = moved + from_right[c, band, :] * jnp.where(last, after[2], here[2])
            moved = moved + (down_v[c, above, :] * t[c, above, :] + up_v[c, below, :] * t[c, below, :])
            put(c, keep_s[c, band, :] * here[0] + moved)
            before, here = here, after

    top, end = HALO, HALO + rows
    later = ITERS - half_way - 1
    path = ((1, 0, 2), (4, 3, 5))

    def substep(advance, source, target, starts):
        for start in starts:

            def put(c, new):
                states[target][c, pl.ds(start, TILE), :] = new

            advance(states[source], start, put)

    def middle_copy(i, down):
        start = end - half_way if down else top
        return pltpu.make_async_remote_copy(
            src_ref=fields.at[path[i][0], :, pl.ds(start, half_way), :],
            dst_ref=middle.at[0 if down else 1, i],
            send_sem=halo_sem.at[4 + 2 * i + (0 if down else 1)],
            recv_sem=halo_sem.at[8 + 2 * i + (0 if down else 1)],
            device_id={"tile": lax.rem(me + (1 if down else n - 1), n)},
            device_id_type=MESH,
        )

    def first_half(i, advance):
        source, target = 3 * i, 3 * i + 1
        for reach in range(half_way - 1, 0, -1):
            substep(advance, source, target, range(top - reach, end + reach, TILE))
            source, target = target, source
        substep(advance, source, target, (top, end - TILE))

        @pl.when(me < n - 1)
        def _():
            middle_copy(i, True).start()

        @pl.when(me > 0)
        def _():
            middle_copy(i, False).start()

        substep(advance, source, target, range(top + TILE, end - TILE, TILE))

    def take_middle(i):
        @pl.when(me > 0)
        def _():
            middle_copy(i, True).wait_recv()

        @pl.when(me < n - 1)
        def _():
            middle_copy(i, False).wait_recv()

        for c in range(chunks):
            states[path[i][0]][c, top - half_way : top, :] = middle[0, i, c]
            states[path[i][0]][c, end : end + half_way, :] = middle[1, i, c]

    def edges(i, advance):
        for q in range(later):
            reach = later - q
            substep(advance, path[i][q], path[i][q + 1], (top - reach, end - TILE + reach))

    def last_water(starts):
        for start in starts:
            band = pl.ds(start - HALO, TILE)

            def put(c, new):
                final[c, band, :] = new
                taken = new * ratio[c, band, :]
                high = taken.astype(jnp.bfloat16).astype(jnp.float32)
                high_v[c, band, :] = high
                rest_v[c, band, :] = taken - high

            advance_water(states[path[0][later]], start, put)

    def last_store(starts):
        for start in starts:
            band = pl.ds(start - HALO, TILE)

            def put(c, new):
                sub_out[band, at(c)] = new

            advance_store(states[path[1][later]], start, put)

    first_half(0, advance_water)
    for q in range(later):
        substep(advance_water, path[0][q], path[0][q + 1], range(top + 2 * q, end, TILE))
    last_water((*range(top + half_way, end - half_way - TILE, TILE), end - half_way - TILE))

    def add_row(r, total):
        hot = owner_hot[r]
        left = []
        for ref in (high_v, rest_v):
            row = jnp.concatenate([row_of(ref, c, r) for c in range(chunks)], axis=1)
            left += [hot[16 * q : 16 * (q + 1)] * row for q in range(n // 16)]
        left = jnp.concatenate(left, axis=0)
        return total + lax.dot_general(left, spot_hot[r], NT, preferred_element_type=jnp.float32)

    total = jnp.zeros((2 * n, per_owner), jnp.float32)
    inside = rows // 2
    total = lax.fori_loop(half_way + 1, half_way + 1 + inside, add_row, total, unroll=8)
    take_middle(0)
    edges(0, advance_water)
    last_water((top, end - TILE))

    def add_wrapped(r, total):
        return add_row(lax.rem(r, rows), total)

    total = lax.fori_loop(half_way + 1 + inside, half_way + 1 + rows, add_wrapped, total, unroll=8)
    sums = total[:n] + total[n:]
    sums = jnp.concatenate([sums] * twins, axis=1)
    for k in range(n):
        sums_send[k] = sums[k : k + 1, :]
    sums_recv[me] = sums_send[me]
    to_peers(2, lambda peer: sums_send.at[peer], sums_recv.at[me])

    for m in (*outer, *inner):
        fill(m, 1)
    first_half(1, advance_store)
    for q in range(later):
        reach = later - q
        substep(advance_store, path[1][q], path[1][q + 1], range(top + TILE - reach, end - TILE + reach, TILE))
    last_store(range(top + TILE, end - TILE, TILE))
    for m in range(rows // TILE):
        band = pl.ds(TILE * m, TILE)
        for c in range(chunks):
            depth = final[c, band, :] * inverse[c, band, :]
            head_out[band, at(c)] = depth - share_v[band, at(c)] * depth

    drain(places.at[pl.ds(0, n - 1)], a2a_send.at[1])
    drain(places.at[pl.ds(0, n - 1)], a2a_recv.at[1])
    half = lax.broadcasted_iota(jnp.int32, (1, LANES), 1) // per_owner == lax.rem(me, twins)
    lane_line = lax.broadcasted_iota(jnp.int32, (LANES, LANES), 0)
    reach_line = lax.broadcasted_iota(jnp.int32, (reach_rows, LANES), 0)
    for j in range(n):
        low = lax.rem(places[j], LANES)
        spots[:, at(j)] = jnp.where(half & (lane_line == low), 1.0, 0.0).astype(jnp.bfloat16)

    take_middle(1)
    edges(1, advance_store)
    last_store((top, end - TILE))

    @pl.when(me < n - 1)
    def _():
        drain(halo_bytes, halo_sem.at[0])
        middle_copy(0, True).wait_send()
        middle_copy(1, True).wait_send()

    @pl.when(me > 0)
    def _():
        drain(halo_bytes, halo_sem.at[1])
        middle_copy(0, False).wait_send()
        middle_copy(1, False).wait_send()

    drain(sums_send.at[pl.ds(0, n - 1)], a2a_send.at[2])
    drain(sums_send.at[pl.ds(0, n - 1)], a2a_recv.at[2])
    found = []
    for j in range(n):
        high = places[j] // LANES
        found.append(jnp.where(reach_line == high, sums_recv[j], 0.0))
    found = jnp.concatenate(parts_of(jnp.concatenate(found, axis=1), 3), axis=0)
    reach = lax.dot_general(found, spots[...], NT, preferred_element_type=jnp.float32)
    reach_out[...] = reach[:reach_rows] + reach[reach_rows : 2 * reach_rows] + reach[2 * reach_rows :]


def flush(*refs):
    count = (len(refs) - 1) // 2
    copies = [
        pltpu.make_async_copy(src, dst, refs[-1].at[i])
        for i, (src, dst) in enumerate(zip(refs[:count], refs[count:-1]))
    ]
    for copy in copies:
        copy.start()
    for copy in copies:
        copy.wait()


def local(*args):
    n = lax.axis_size("tile")
    precip, head_init, slot_reach = args[0], args[5], args[12]
    cols, land_rows = precip.shape
    rows, width = head_init.shape
    slots = slot_reach.shape[0]
    full = rows + 2 * HALO
    land_dev = land_rows // n
    per_chunk = LANES // (width // n)
    chunks = width // LANES
    per_owner = slots // n
    f32, i32, b16 = jnp.float32, jnp.int32, jnp.bfloat16
    tall = pltpu.VMEM((full, width), f32)
    anywhere = pl.BlockSpec(memory_space=pl.ANY)
    soil, head, sub, reach = pl.pallas_call(
        functools.partial(kernel, n),
        out_shape=(
            pltpu.VMEM(precip.shape, f32),
            pltpu.VMEM(head_init.shape, f32),
            pltpu.VMEM(head_init.shape, f32),
            pltpu.VMEM((slots // LANES, LANES), f32),
        ),
        in_specs=[anywhere] * 13,
        out_specs=(pl.BlockSpec(memory_space=pltpu.VMEM),) * 4,
        scratch_shapes=[
            pltpu.VMEM((4, cols, land_rows), f32),
            pltpu.VMEM((cols, land_rows), i32),
            pltpu.VMEM((LANES, land_rows), f32),
            pltpu.VMEM((n, land_dev, LANES), f32),
            pltpu.VMEM((per_chunk, chunks, land_dev, LANES), f32),
            pltpu.VMEM((chunks * land_dev, 4 * LANES), f32),
            tall,
            tall,
            tall,
            tall,
            pltpu.VMEM((full, width), i32),
            pltpu.VMEM((rows, width), f32),
            pltpu.VMEM((rows, width), i32),
            pltpu.VMEM((6, chunks, full + TILE, LANES), f32),
            pltpu.VMEM((9, chunks, full + TILE, LANES), f32),
            pltpu.VMEM((chunks, rows, LANES), f32),
            pltpu.VMEM((chunks, rows, LANES), f32),
            pltpu.VMEM((chunks, rows, LANES), f32),
            pltpu.VMEM((2, chunks, rows + TILE, LANES), f32),
            pltpu.VMEM((2, chunks, rows + TILE, LANES), f32),
            pltpu.VMEM((rows, n, width), b16),
            pltpu.VMEM((rows, per_owner, width), b16),
            pltpu.VMEM((n, 1, LANES), f32),
            pltpu.VMEM((n, 1, LANES), f32),
            pltpu.VMEM((n, 1, LANES), i32),
            pltpu.VMEM((LANES, n * LANES), b16),
            pltpu.VMEM((2, 2, chunks, ITERS // 2, LANES), f32),
            pltpu.SemaphoreType.DMA((2,)),
            pltpu.SemaphoreType.DMA((8,)),
            pltpu.SemaphoreType.DMA((12,)),
            pltpu.SemaphoreType.DMA((3,)),
            pltpu.SemaphoreType.DMA((3,)),
        ],
        compiler_params=pltpu.CompilerParams(
            collective_id=0,
            has_side_effects=True,
            vmem_limit_bytes=40 * 2**20,
        ),
        name="step",
    )(*[pltpu.with_memory_space_constraint(x, pltpu.HBM) for x in (*args[:12], slot_reach.reshape(slots // LANES, 1, LANES))])
    results = (soil, head, sub, reach)
    soil, head, sub, reach = pl.pallas_call(
        flush,
        out_shape=tuple(jax.ShapeDtypeStruct(x.shape, x.dtype) for x in results),
        in_specs=[pl.BlockSpec(memory_space=pltpu.VMEM)] * 4,
        out_specs=(anywhere,) * 4,
        scratch_shapes=[pltpu.SemaphoreType.DMA((4,))],
        compiler_params=pltpu.CompilerParams(vmem_limit_bytes=2**20),
        name="flush",
    )(*results)
    return soil, head, sub, reach.reshape(slots)


def solution(mesh):
    grid = P(("member", "tile"), None)
    line = P(("member", "tile"))
    return jax.shard_map(
        local,
        mesh=mesh,
        in_specs=(grid,) * 12 + (line,),
        out_specs=(grid, grid, grid, line),
        check_vma=False,
    )
```

```python
import functools

import jax
import jax.numpy as jnp
from jax import lax
from jax.experimental import pallas as pl
from jax.experimental.pallas import tpu as pltpu
from jax.sharding import PartitionSpec as P

ITERS = 6
HALO = 8
TILE = 8
LANES = 128
MESH = pl.DeviceIdType.MESH
NT = (((1,), (1,)), ((), ()))


def parts_of(x, count):
    parts = []
    for _ in range(count):
        part = x.astype(jnp.bfloat16)
        parts.append(part)
        x = x - part.astype(jnp.float32)
    return parts


def kernel(
    n,
    precip,
    pet,
    soil_init,
    ksat,
    land_mask,
    head_init,
    subsurface_init,
    conduct,
    drain_rate,
    flow_code,
    channel_share,
    cell_slot,
    slot_reach,
    soil_out,
    head_out,
    sub_out,
    reach_out,
    land_in,
    mask_in,
    pack,
    land_send,
    land_recv,
    wide,
    h,
    s,
    g,
    d,
    code,
    share_v,
    slot_v,
    fields,
    statics,
    inverse,
    ratio,
    final,
    values,
    keys,
    owner_hot,
    spot_hot,
    sums_send,
    sums_recv,
    places,
    spots,
    middle,
    land_sem,
    own_sem,
    halo_sem,
    a2a_send,
    a2a_recv,
):
    me = lax.axis_index("tile")
    cols, land_rows = precip.shape
    rows, width = head_init.shape
    full = rows + 2 * HALO
    chunks = width // LANES
    land_dev = land_rows // n
    per_chunk = LANES // (width // n)
    per_owner = slot_reach.shape[0] * LANES // n
    twins = LANES // per_owner
    reach_rows = reach_out.shape[0]
    tall = ((head_init, h), (conduct, g), (subsurface_init, s), (drain_rate, d), (flow_code, code))
    urgent, patient = (0, 1), (2, 3, 4)
    states = [fields.at[i] for i in range(6)]
    water, store = states[0], states[3]
    half_way = ITERS // 2
    cond, sides, square, keep_h, keep_s, down_v, up_v, from_left, from_right = (
        statics.at[i] for i in range(9)
    )
    high_v, rest_v = values.at[0], values.at[1]
    owner_v, spot_v = keys.at[0], keys.at[1]

    land_copies = [
        pltpu.make_async_copy(ref, land_in.at[i], land_sem.at[0])
        for i, ref in enumerate((precip, pet, soil_init, ksat))
    ]
    land_copies.append(pltpu.make_async_copy(land_mask, mask_in, land_sem.at[1]))
    for copy in land_copies:
        copy.start()

    barrier = pltpu.get_barrier_semaphore()
    for k in range(1, n):
        pl.semaphore_signal(
            barrier, inc=1, device_id={"tile": lax.rem(me + k, n)}, device_id_type=MESH
        )

    own = [
        pltpu.make_async_copy(src, dst.at[pl.ds(HALO, rows)], own_sem.at[i])
        for i, (src, dst) in enumerate(tall)
    ]
    own.append(pltpu.make_async_copy(channel_share, share_v, own_sem.at[5]))
    own.append(pltpu.make_async_copy(cell_slot, slot_v, own_sem.at[6]))
    own.append(pltpu.make_async_copy(slot_reach.at[me // twins], places.at[me], own_sem.at[7]))
    for copy in own:
        copy.start()

    @pl.when(me == 0)
    def _():
        for _, dst in tall:
            dst[:HALO, :] = jnp.zeros((HALO, width), dst.dtype)
        middle[0] = jnp.zeros(middle.shape[1:], jnp.float32)

    @pl.when(me == n - 1)
    def _():
        for _, dst in tall:
            dst[full - HALO :, :] = jnp.zeros((HALO, width), dst.dtype)
        middle[1] = jnp.zeros(middle.shape[1:], jnp.float32)

    land_copies[-1].wait()
    pltpu.make_async_copy(land_in, land_in, land_sem.at[0]).wait()
    rain, demand, moist, conductivity = land_in[0], land_in[1], land_in[2], land_in[3]
    mask = mask_in[...].astype(jnp.float32)
    wet = 2.0 * moist
    cap = conductivity * (1.0 - wet)
    runoff = mask * rain * rain / (rain + cap)
    drainage = 0.25 * mask * conductivity * (wet * wet) * (wet * wet)
    evap = mask * demand * wet
    soil_out[...] = moist + 0.1 * (mask * rain - runoff - drainage - evap)
    lane = lax.broadcasted_iota(jnp.int32, (cols, land_rows), 1)
    place = lax.rem(lane, land_dev)
    side = HALO // 4
    if 4 * cols < LANES:
        pack[4 * cols :, :] = jnp.zeros((LANES - 4 * cols, land_rows), jnp.float32)
    for i, x in enumerate((runoff, drainage)):
        pack[i * cols : (i + 1) * cols, :] = x
        before = jnp.where(lane >= land_dev, pltpu.roll(x, side, 1), 0.0)
        after = jnp.where(
            lane < land_rows - land_dev, pltpu.roll(x, land_rows - (land_dev - side), 1), 0.0
        )
        pack[(2 + i) * cols : (3 + i) * cols, :] = jnp.where(place < side, before, after)
    land_send[...] = jnp.transpose(pack[...]).reshape(n, land_dev, LANES)

    def drain(ref, sem):
        pltpu.make_async_copy(ref, ref, sem).wait()

    def to_peers(stage, source, target):
        for k in range(1, n):
            peer = lax.rem(me + jnp.where(me < n // 2, n - k, k), n)
            pltpu.make_async_remote_copy(
                src_ref=source(peer),
                dst_ref=target,
                send_sem=a2a_send.at[stage],
                recv_sem=a2a_recv.at[stage],
                device_id={"tile": peer},
                device_id_type=MESH,
            ).start()

    def at(c):
        return pl.ds(c * LANES, LANES)

    lane8 = lax.broadcasted_iota(jnp.int32, (TILE, LANES), 1)
    first = lane8 == 0
    last = lane8 == LANES - 1
    top8 = lax.broadcasted_iota(jnp.int32, (TILE, LANES), 0) < TILE // 2
    zero = jnp.zeros((TILE, LANES), jnp.float32)

    def rolled(x):
        return (pltpu.roll(x, 1, 1), pltpu.roll(x, LANES - 1, 1))

    def prepare_water(m):
        band = pl.ds(TILE * m, TILE)

        def load(c):
            gc = g[band, at(c)]
            cond[c, band, :] = gc
            square[c, band, :] = gc * gc
            return rolled(gc)

        before, here = (zero,) * 2, load(0)
        for c in range(chunks):
            after = load(c + 1) if c + 1 < chunks else (zero,) * 2
            sides[c, band, :] = jnp.where(first, before[0], here[0]) + jnp.where(last, after[1], here[1])
            before, here = here, after

    def prepare_store(m):
        band = pl.ds(TILE * m, TILE)

        def load(c):
            dc, kc = d[band, at(c)], code[band, at(c)]
            down, up, right, left = (jnp.where(kc == q, dc, 0.0) for q in range(4))
            keep_s[c, band, :] = 1.0 - (down + up + right + left)
            down_v[c, band, :] = down
            up_v[c, band, :] = up
            return (pltpu.roll(right, 1, 1), pltpu.roll(left, LANES - 1, 1))

        before, here = (zero,) * 2, load(0)
        for c in range(chunks):
            after = load(c + 1) if c + 1 < chunks else (zero,) * 2
            from_left[c, band, :] = jnp.where(first, before[0], here[0])
            from_right[c, band, :] = jnp.where(last, after[1], here[1])
            before, here = here, after

    def finish(start):
        band, above, below = (pl.ds(start + q, TILE) for q in (0, -1, 1))
        for c in range(chunks):
            around = (cond[c, above, :] + cond[c, below, :]) + sides[c, band, :]
            keep_h[c, band, :] = 1.0 - cond[c, band, :] * around

    line = lax.broadcasted_iota(jnp.int32, (16, LANES), 0).astype(jnp.float32)
    lines = [(line + 16 * q).astype(jnp.bfloat16) for q in range(max(n, per_owner) // 16)]
    one, none = jnp.ones((16, LANES), jnp.bfloat16), jnp.zeros((16, LANES), jnp.bfloat16)

    def row_of(ref, c, r):
        half = ref[c, pl.ds(r, TILE, stride=0), :]
        return jnp.concatenate([half, half], axis=0).astype(jnp.bfloat16)

    def make_hot(r, carry):
        for ref, hot, count in ((owner_v, owner_hot, n), (spot_v, spot_hot, per_owner)):
            for c in range(chunks):
                key = row_of(ref, c, r)
                for q in range(count // 16):
                    hot[r, 16 * q : 16 * (q + 1), at(c)] = jnp.where(key == lines[q], one, none)
        return carry

    inner = range(1, 1 + rows // TILE)

    def local_work():
        for copy in own:
            copy.wait()
        for m in inner:
            prepare_water(m)
            prepare_store(m)
            band, own_band = pl.ds(TILE * m, TILE), pl.ds(TILE * (m - 1), TILE)
            for c in range(chunks):
                backward = 1.0 / g[band, at(c)]
                inverse[c, own_band, :] = backward
                ratio[c, own_band, :] = share_v[own_band, at(c)] * backward
                slot = slot_v[own_band, at(c)]
                owner = slot // per_owner
                owner_v[c, own_band, :] = owner.astype(jnp.float32)
                spot_v[c, own_band, :] = (slot - owner * per_owner).astype(jnp.float32)
        for start in (*range(HALO + 1, HALO + rows - TILE, TILE), HALO + rows - TILE - 1):
            finish(start)
        lax.fori_loop(0, rows, make_hot, 0)

    @pl.when(me < n // 2)
    def _():
        local_work()

    pl.semaphore_wait(barrier, n - 1)
    own_land = land_recv.at[lax.rem(me, per_chunk), me // per_chunk]
    to_peers(0, lambda peer: land_send.at[peer], own_land)

    def halo_copy(i, up):
        src, dst = tall[i]
        if up:
            start, land, peer = (rows - half_way, HALO - half_way, me + 1)
        else:
            start, land, peer = (0, full - HALO, me - 1)
        return pltpu.make_async_remote_copy(
            src_ref=src.at[pl.ds(start, half_way)],
            dst_ref=dst.at[pl.ds(land, half_way)],
            send_sem=halo_sem.at[(0 if up else 1) + (0 if i in urgent else 12)],
            recv_sem=halo_sem.at[(2 if up else 3) + (0 if i in urgent else 12)],
            device_id={"tile": lax.rem(peer + n, n)},
            device_id_type=MESH,
        )

    def send_halo(which):
        @pl.when(me < n - 1)
        def _():
            for i in which:
                halo_copy(i, True).start()

        @pl.when(me > 0)
        def _():
            for i in which:
                halo_copy(i, False).start()

    send_halo(urgent)
    send_halo(patient)
    to_peers(1, lambda peer: slot_reach.at[peer // twins], places.at[me])
    land_recv[lax.rem(me, per_chunk), me // per_chunk] = land_send[me]

    @pl.when(me >= n // 2)
    def _():
        local_work()

    def take_halo(which):
        shift = 0 if which is urgent else 12
        size = water.at[:, pl.ds(0, len(which) * half_way), :]

        @pl.when(me > 0)
        def _():
            drain(size, halo_sem.at[2 + shift])

        @pl.when(me < n - 1)
        def _():
            drain(size, halo_sem.at[3 + shift])

    take_halo(urgent)
    outer = (0, full // TILE - 1)
    for m in outer:
        prepare_water(m)
    for start in (1, HALO + rows - 1):
        finish(start)

    drain(land_send.at[pl.ds(0, n - 1)], a2a_send.at[0])
    drain(land_send.at[pl.ds(0, n - 1)], a2a_recv.at[0])

    l_iota = lax.broadcasted_iota(jnp.int32, (LANES, 4 * LANES), 0)
    f_iota = lax.broadcasted_iota(jnp.int32, (LANES, 4 * LANES), 1)
    cell = lax.rem(f_iota, LANES) // 4
    group = f_iota // LANES
    total = None
    for k in range(per_chunk):
        inside = (cell >= k * cols) & (cell < (k + 1) * cols)
        spread = inside & (l_iota == group * cols + cell - k * cols)
        spread = jnp.where(spread, 1.0, 0.0).astype(jnp.bfloat16)
        block = land_recv[k].reshape(chunks * land_dev, LANES)
        for part in parts_of(block, 3):
            term = jnp.dot(part, spread, preferred_element_type=jnp.float32)
            total = term if total is None else total + term
    wide[...] = total

    def fill(m, i):
        band = pl.ds(TILE * m, TILE)
        for c in range(chunks):
            pair = []
            for q in (2 * m, 2 * m + 1):
                if q < side:
                    lanes, r = (2 + i) * LANES, q
                elif q < side + land_dev:
                    lanes, r = i * LANES, q - side
                else:
                    lanes, r = (2 + i) * LANES, q - land_dev
                r = c * land_dev + r
                pair.append(jnp.broadcast_to(wide[r : r + 1, lanes : lanes + LANES], (TILE, LANES)))
            added = jnp.where(top8, pair[0], pair[1])
            if i == 0:
                water[c, band, :] = g[band, at(c)] * (h[band, at(c)] + added)
            else:
                store[c, band, :] = s[band, at(c)] + added

    for m in (*outer, *inner):
        fill(m, 0)

    def advance_water(w, start, put):
        def load(c):
            wc = w[c, pl.ds(start, TILE), :]
            return (wc,) + rolled(wc)

        band, above, below = (pl.ds(start + q, TILE) for q in (0, -1, 1))
        before, here = (zero,) * 3, load(0)
        for c in range(chunks):
            after = load(c + 1) if c + 1 < chunks else (zero,) * 3
            flux = jnp.where(first, before[1], here[1]) + jnp.where(last, after[2], here[2])
            flux = flux + (w[c, above, :] + w[c, below, :])
            put(c, keep_h[c, band, :] * here[0] + square[c, band, :] * flux)
            before, here = here, after

    def advance_store(t, start, put):
        def load(c):
            tc = t[c, pl.ds(start, TILE), :]
            return (tc,) + rolled(tc)

        band, above, below = (pl.ds(start + q, TILE) for q in (0, -1, 1))
        before, here = (zero,) * 3, load(0)
        for c in range(chunks):
            after = load(c + 1) if c + 1 < chunks else (zero,) * 3
            moved = from_left[c, band, :] * jnp.where(first, before[1], here[1])
            moved = moved + from_right[c, band, :] * jnp.where(last, after[2], here[2])
            moved = moved + (down_v[c, above, :] * t[c, above, :] + up_v[c, below, :] * t[c, below, :])
            put(c, keep_s[c, band, :] * here[0] + moved)
            before, here = here, after

    top, end = HALO, HALO + rows
    later = ITERS - half_way - 1
    path = ((1, 0, 2), (4, 3, 5))

    def substep(advance, source, target, starts):
        for start in starts:

            def put(c, new):
                states[target][c, pl.ds(start, TILE), :] = new

            advance(states[source], start, put)

    def middle_copy(i, down):
        start = end - half_way if down else top
        return pltpu.make_async_remote_copy(
            src_ref=fields.at[path[i][0], :, pl.ds(start, half_way), :],
            dst_ref=middle.at[0 if down else 1, i],
            send_sem=halo_sem.at[4 + 2 * i + (0 if down else 1)],
            recv_sem=halo_sem.at[8 + 2 * i + (0 if down else 1)],
            device_id={"tile": lax.rem(me + (1 if down else n - 1), n)},
            device_id_type=MESH,
        )

    def first_half(i, advance):
        source, target = 3 * i, 3 * i + 1
        for reach in range(half_way - 1, 0, -1):
            substep(advance, source, target, range(top - reach, end + reach, TILE))
            source, target = target, source
        substep(advance, source, target, (top, end - TILE))

        @pl.when(me < n - 1)
        def _():
            middle_copy(i, True).start()

        @pl.when(me > 0)
        def _():
            middle_copy(i, False).start()

        substep(advance, source, target, range(top + TILE, end - TILE, TILE))

    def take_middle(i):
        @pl.when(me > 0)
        def _():
            middle_copy(i, True).wait_recv()

        @pl.when(me < n - 1)
        def _():
            middle_copy(i, False).wait_recv()

        for c in range(chunks):
            states[path[i][0]][c, top - half_way : top, :] = middle[0, i, c]
            states[path[i][0]][c, end : end + half_way, :] = middle[1, i, c]

    def edges(i, advance):
        for q in range(later):
            reach = later - q
            substep(advance, path[i][q], path[i][q + 1], (top - reach, end - TILE + reach))

    def last_water(starts):
        for start in starts:
            band = pl.ds(start - HALO, TILE)

            def put(c, new):
                final[c, band, :] = new
                taken = new * ratio[c, band, :]
                high = taken.astype(jnp.bfloat16).astype(jnp.float32)
                high_v[c, band, :] = high
                rest_v[c, band, :] = taken - high

            advance_water(states[path[0][later]], start, put)

    def last_store(starts):
        for start in starts:
            band = pl.ds(start - HALO, TILE)

            def put(c, new):
                sub_out[band, at(c)] = new

            advance_store(states[path[1][later]], start, put)

    first_half(0, advance_water)
    for q in range(later):
        reach = later - q
        substep(advance_water, path[0][q], path[0][q + 1], range(top + TILE - reach, end - TILE + reach, TILE))
    last_water(range(top + TILE, end - TILE, TILE))

    def add_row(r, total):
        hot = owner_hot[r]
        left = []
        for ref in (high_v, rest_v):
            row = jnp.concatenate([row_of(ref, c, r) for c in range(chunks)], axis=1)
            left += [hot[16 * q : 16 * (q + 1)] * row for q in range(n // 16)]
        left = jnp.concatenate(left, axis=0)
        return total + lax.dot_general(left, spot_hot[r], NT, preferred_element_type=jnp.float32)

    total = jnp.zeros((2 * n, per_owner), jnp.float32)
    total = lax.fori_loop(TILE, rows - TILE, add_row, total, unroll=8)
    take_middle(0)
    edges(0, advance_water)
    last_water((top, end - TILE))

    def add_wrapped(r, total):
        return add_row(lax.rem(r, rows), total)

    total = lax.fori_loop(rows - TILE, rows + TILE, add_wrapped, total, unroll=8)
    sums = total[:n] + total[n:]
    sums = jnp.concatenate([sums] * twins, axis=1)
    for k in range(n):
        sums_send[k] = sums[k : k + 1, :]
    sums_recv[me] = sums_send[me]
    to_peers(2, lambda peer: sums_send.at[peer], sums_recv.at[me])

    take_halo(patient)
    for m in outer:
        prepare_store(m)
    for m in (*outer, *inner):
        fill(m, 1)
    first_half(1, advance_store)
    for q in range(later):
        reach = later - q
        substep(advance_store, path[1][q], path[1][q + 1], range(top + TILE - reach, end - TILE + reach, TILE))
    last_store(range(top + TILE, end - TILE, TILE))
    for m in range(rows // TILE):
        band = pl.ds(TILE * m, TILE)
        for c in range(chunks):
            depth = final[c, band, :] * inverse[c, band, :]
            head_out[band, at(c)] = depth - share_v[band, at(c)] * depth

    drain(places.at[pl.ds(0, n - 1)], a2a_send.at[1])
    drain(places.at[pl.ds(0, n - 1)], a2a_recv.at[1])
    half = lax.broadcasted_iota(jnp.int32, (1, LANES), 1) // per_owner == lax.rem(me, twins)
    lane_line = lax.broadcasted_iota(jnp.int32, (LANES, LANES), 0)
    reach_line = lax.broadcasted_iota(jnp.int32, (reach_rows, LANES), 0)
    for j in range(n):
        low = lax.rem(places[j], LANES)
        spots[:, at(j)] = jnp.where(half & (lane_line == low), 1.0, 0.0).astype(jnp.bfloat16)

    take_middle(1)
    edges(1, advance_store)
    last_store((top, end - TILE))

    @pl.when(me < n - 1)
    def _():
        drain(water.at[:, pl.ds(0, len(urgent) * half_way), :], halo_sem.at[0])
        drain(water.at[:, pl.ds(0, len(patient) * half_way), :], halo_sem.at[12])
        middle_copy(0, True).wait_send()
        middle_copy(1, True).wait_send()

    @pl.when(me > 0)
    def _():
        drain(water.at[:, pl.ds(0, len(urgent) * half_way), :], halo_sem.at[1])
        drain(water.at[:, pl.ds(0, len(patient) * half_way), :], halo_sem.at[13])
        middle_copy(0, False).wait_send()
        middle_copy(1, False).wait_send()

    drain(sums_send.at[pl.ds(0, n - 1)], a2a_send.at[2])
    drain(sums_send.at[pl.ds(0, n - 1)], a2a_recv.at[2])
    found = []
    for j in range(n):
        high = places[j] // LANES
        found.append(jnp.where(reach_line == high, sums_recv[j], 0.0))
    found = jnp.concatenate(parts_of(jnp.concatenate(found, axis=1), 3), axis=0)
    reach = lax.dot_general(found, spots[...], NT, preferred_element_type=jnp.float32)
    reach_out[...] = reach[:reach_rows] + reach[reach_rows : 2 * reach_rows] + reach[2 * reach_rows :]


def flush(*refs):
    count = (len(refs) - 1) // 2
    copies = [
        pltpu.make_async_copy(src, dst, refs[-1].at[i])
        for i, (src, dst) in enumerate(zip(refs[:count], refs[count:-1]))
    ]
    for copy in copies:
        copy.start()
    for copy in copies:
        copy.wait()


def local(*args):
    n = lax.axis_size("tile")
    precip, head_init, slot_reach = args[0], args[5], args[12]
    cols, land_rows = precip.shape
    rows, width = head_init.shape
    slots = slot_reach.shape[0]
    full = rows + 2 * HALO
    land_dev = land_rows // n
    per_chunk = LANES // (width // n)
    chunks = width // LANES
    per_owner = slots // n
    f32, i32, b16 = jnp.float32, jnp.int32, jnp.bfloat16
    tall = pltpu.VMEM((full, width), f32)
    anywhere = pl.BlockSpec(memory_space=pl.ANY)
    soil, head, sub, reach = pl.pallas_call(
        functools.partial(kernel, n),
        out_shape=(
            pltpu.VMEM(precip.shape, f32),
            pltpu.VMEM(head_init.shape, f32),
            pltpu.VMEM(head_init.shape, f32),
            pltpu.VMEM((slots // LANES, LANES), f32),
        ),
        in_specs=[anywhere] * 13,
        out_specs=(pl.BlockSpec(memory_space=pltpu.VMEM),) * 4,
        scratch_shapes=[
            pltpu.VMEM((4, cols, land_rows), f32),
            pltpu.VMEM((cols, land_rows), i32),
            pltpu.VMEM((LANES, land_rows), f32),
            pltpu.VMEM((n, land_dev, LANES), f32),
            pltpu.VMEM((per_chunk, chunks, land_dev, LANES), f32),
            pltpu.VMEM((chunks * land_dev, 4 * LANES), f32),
            tall,
            tall,
            tall,
            tall,
            pltpu.VMEM((full, width), i32),
            pltpu.VMEM((rows, width), f32),
            pltpu.VMEM((rows, width), i32),
            pltpu.VMEM((6, chunks, full + TILE, LANES), f32),
            pltpu.VMEM((9, chunks, full + TILE, LANES), f32),
            pltpu.VMEM((chunks, rows, LANES), f32),
            pltpu.VMEM((chunks, rows, LANES), f32),
            pltpu.VMEM((chunks, rows, LANES), f32),
            pltpu.VMEM((2, chunks, rows + TILE, LANES), f32),
            pltpu.VMEM((2, chunks, rows + TILE, LANES), f32),
            pltpu.VMEM((rows, n, width), b16),
            pltpu.VMEM((rows, per_owner, width), b16),
            pltpu.VMEM((n, 1, LANES), f32),
            pltpu.VMEM((n, 1, LANES), f32),
            pltpu.VMEM((n, 1, LANES), i32),
            pltpu.VMEM((LANES, n * LANES), b16),
            pltpu.VMEM((2, 2, chunks, ITERS // 2, LANES), f32),
            pltpu.SemaphoreType.DMA((2,)),
            pltpu.SemaphoreType.DMA((8,)),
            pltpu.SemaphoreType.DMA((16,)),
            pltpu.SemaphoreType.DMA((3,)),
            pltpu.SemaphoreType.DMA((3,)),
        ],
        compiler_params=pltpu.CompilerParams(
            collective_id=0,
            has_side_effects=True,
            vmem_limit_bytes=40 * 2**20,
        ),
        name="step",
    )(*[pltpu.with_memory_space_constraint(x, pltpu.HBM) for x in (*args[:12], slot_reach.reshape(slots // LANES, 1, LANES))])
    results = (soil, head, sub, reach)
    soil, head, sub, reach = pl.pallas_call(
        flush,
        out_shape=tuple(jax.ShapeDtypeStruct(x.shape, x.dtype) for x in results),
        in_specs=[pl.BlockSpec(memory_space=pltpu.VMEM)] * 4,
        out_specs=(anywhere,) * 4,
        scratch_shapes=[pltpu.SemaphoreType.DMA((4,))],
        compiler_params=pltpu.CompilerParams(vmem_limit_bytes=2**20),
        name="flush",
    )(*results)
    return soil, head, sub, reach.reshape(slots)


def solution(mesh):
    grid = P(("member", "tile"), None)
    line = P(("member", "tile"))
    return jax.shard_map(
        local,
        mesh=mesh,
        in_specs=(grid,) * 12 + (line,),
        out_specs=(grid, grid, grid, line),
        check_vma=False,
    )
```

```python
import functools

import jax
import jax.numpy as jnp
from jax import lax
from jax.experimental import pallas as pl
from jax.experimental.pallas import tpu as pltpu
from jax.sharding import PartitionSpec as P

ITERS = 6
HALO = 8
TILE = 8
LANES = 128
MESH = pl.DeviceIdType.MESH
NT = (((1,), (1,)), ((), ()))


def parts_of(x, count):
    parts = []
    for _ in range(count):
        part = x.astype(jnp.bfloat16)
        parts.append(part)
        x = x - part.astype(jnp.float32)
    return parts


def kernel(
    n,
    precip,
    pet,
    soil_init,
    ksat,
    land_mask,
    head_init,
    subsurface_init,
    conduct,
    drain_rate,
    flow_code,
    channel_share,
    cell_slot,
    slot_reach,
    soil_out,
    head_out,
    sub_out,
    sums_recv,
    places,
    spots,
    land_in,
    mask_in,
    pack,
    land_send,
    land_recv,
    wide,
    h,
    s,
    g,
    d,
    code,
    share_v,
    slot_v,
    fields,
    statics,
    inverse,
    ratio,
    final,
    values,
    keys,
    owner_hot,
    spot_hot,
    sums_send,
    middle,
    land_sem,
    own_sem,
    halo_sem,
    a2a_send,
    a2a_recv,
):
    me = lax.axis_index("tile")
    cols, land_rows = precip.shape
    rows, width = head_init.shape
    full = rows + 2 * HALO
    chunks = width // LANES
    land_dev = land_rows // n
    per_chunk = LANES // (width // n)
    per_owner = slot_reach.shape[0] * LANES // n
    twins = LANES // per_owner
    tall = ((head_init, h), (conduct, g), (subsurface_init, s), (drain_rate, d), (flow_code, code))
    urgent, patient = (0, 1), (2, 3, 4)
    states = [fields.at[i] for i in range(6)]
    water, store = states[0], states[3]
    half_way = ITERS // 2
    cond, sides, square, keep_h, keep_s, down_v, up_v, from_left, from_right = (
        statics.at[i] for i in range(9)
    )
    high_v, rest_v = values.at[0], values.at[1]
    owner_v, spot_v = keys.at[0], keys.at[1]

    land_copies = [
        pltpu.make_async_copy(ref, land_in.at[i], land_sem.at[0])
        for i, ref in enumerate((precip, pet, soil_init, ksat))
    ]
    land_copies.append(pltpu.make_async_copy(land_mask, mask_in, land_sem.at[1]))
    for copy in land_copies:
        copy.start()

    barrier = pltpu.get_barrier_semaphore()
    for k in range(1, n):
        pl.semaphore_signal(
            barrier, inc=1, device_id={"tile": lax.rem(me + k, n)}, device_id_type=MESH
        )

    own = [
        pltpu.make_async_copy(src, dst.at[pl.ds(HALO, rows)], own_sem.at[i])
        for i, (src, dst) in enumerate(tall)
    ]
    own.append(pltpu.make_async_copy(channel_share, share_v, own_sem.at[5]))
    own.append(pltpu.make_async_copy(cell_slot, slot_v, own_sem.at[6]))
    own.append(pltpu.make_async_copy(slot_reach.at[me // twins], places.at[me], own_sem.at[7]))
    for copy in own:
        copy.start()

    @pl.when(me == 0)
    def _():
        for _, dst in tall:
            dst[:HALO, :] = jnp.zeros((HALO, width), dst.dtype)
        middle[0] = jnp.zeros(middle.shape[1:], jnp.float32)

    @pl.when(me == n - 1)
    def _():
        for _, dst in tall:
            dst[full - HALO :, :] = jnp.zeros((HALO, width), dst.dtype)
        middle[1] = jnp.zeros(middle.shape[1:], jnp.float32)

    land_copies[-1].wait()
    pltpu.make_async_copy(land_in, land_in, land_sem.at[0]).wait()
    rain, demand, moist, conductivity = land_in[0], land_in[1], land_in[2], land_in[3]
    mask = mask_in[...].astype(jnp.float32)
    wet = 2.0 * moist
    cap = conductivity * (1.0 - wet)
    runoff = mask * rain * rain / (rain + cap)
    drainage = 0.25 * mask * conductivity * (wet * wet) * (wet * wet)
    evap = mask * demand * wet
    soil_out[...] = moist + 0.1 * (mask * rain - runoff - drainage - evap)
    lane = lax.broadcasted_iota(jnp.int32, (cols, land_rows), 1)
    place = lax.rem(lane, land_dev)
    side = HALO // 4
    if 4 * cols < LANES:
        pack[4 * cols :, :] = jnp.zeros((LANES - 4 * cols, land_rows), jnp.float32)
    for i, x in enumerate((runoff, drainage)):
        pack[i * cols : (i + 1) * cols, :] = x
        before = jnp.where(lane >= land_dev, pltpu.roll(x, side, 1), 0.0)
        after = jnp.where(
            lane < land_rows - land_dev, pltpu.roll(x, land_rows - (land_dev - side), 1), 0.0
        )
        pack[(2 + i) * cols : (3 + i) * cols, :] = jnp.where(place < side, before, after)
    land_send[...] = jnp.transpose(pack[...]).reshape(n, land_dev, LANES)

    def drain(ref, sem):
        pltpu.make_async_copy(ref, ref, sem).wait()

    def to_peers(stage, source, target):
        for k in range(1, n):
            peer = lax.rem(me + jnp.where(me < n // 2, n - k, k), n)
            pltpu.make_async_remote_copy(
                src_ref=source(peer),
                dst_ref=target,
                send_sem=a2a_send.at[stage],
                recv_sem=a2a_recv.at[stage],
                device_id={"tile": peer},
                device_id_type=MESH,
            ).start()

    def at(c):
        return pl.ds(c * LANES, LANES)

    lane8 = lax.broadcasted_iota(jnp.int32, (TILE, LANES), 1)
    first = lane8 == 0
    last = lane8 == LANES - 1
    top8 = lax.broadcasted_iota(jnp.int32, (TILE, LANES), 0) < TILE // 2
    zero = jnp.zeros((TILE, LANES), jnp.float32)

    def rolled(x):
        return (pltpu.roll(x, 1, 1), pltpu.roll(x, LANES - 1, 1))

    def prepare_water(m):
        band = pl.ds(TILE * m, TILE)

        def load(c):
            gc = g[band, at(c)]
            cond[c, band, :] = gc
            square[c, band, :] = gc * gc
            return rolled(gc)

        before, here = (zero,) * 2, load(0)
        for c in range(chunks):
            after = load(c + 1) if c + 1 < chunks else (zero,) * 2
            sides[c, band, :] = jnp.where(first, before[0], here[0]) + jnp.where(last, after[1], here[1])
            before, here = here, after

    def prepare_store(m):
        band = pl.ds(TILE * m, TILE)

        def load(c):
            dc, kc = d[band, at(c)], code[band, at(c)]
            down, up, right, left = (jnp.where(kc == q, dc, 0.0) for q in range(4))
            keep_s[c, band, :] = 1.0 - (down + up + right + left)
            down_v[c, band, :] = down
            up_v[c, band, :] = up
            return (pltpu.roll(right, 1, 1), pltpu.roll(left, LANES - 1, 1))

        before, here = (zero,) * 2, load(0)
        for c in range(chunks):
            after = load(c + 1) if c + 1 < chunks else (zero,) * 2
            from_left[c, band, :] = jnp.where(first, before[0], here[0])
            from_right[c, band, :] = jnp.where(last, after[1], here[1])
            before, here = here, after

    def finish(start):
        band, above, below = (pl.ds(start + q, TILE) for q in (0, -1, 1))
        for c in range(chunks):
            around = (cond[c, above, :] + cond[c, below, :]) + sides[c, band, :]
            keep_h[c, band, :] = 1.0 - cond[c, band, :] * around

    line = lax.broadcasted_iota(jnp.int32, (16, LANES), 0).astype(jnp.float32)
    lines = [(line + 16 * q).astype(jnp.bfloat16) for q in range(max(n, per_owner) // 16)]
    one, none = jnp.ones((16, LANES), jnp.bfloat16), jnp.zeros((16, LANES), jnp.bfloat16)

    def row_of(ref, c, r):
        half = ref[c, pl.ds(r, TILE, stride=0), :]
        return jnp.concatenate([half, half], axis=0).astype(jnp.bfloat16)

    def make_hot(r, carry):
        for ref, hot, count in ((owner_v, owner_hot, n), (spot_v, spot_hot, per_owner)):
            for c in range(chunks):
                key = row_of(ref, c, r)
                for q in range(count // 16):
                    hot[r, 16 * q : 16 * (q + 1), at(c)] = jnp.where(key == lines[q], one, none)
        return carry

    inner = range(1, 1 + rows // TILE)

    def local_work():
        for copy in own:
            copy.wait()
        for m in inner:
            prepare_water(m)
            prepare_store(m)
            band, own_band = pl.ds(TILE * m, TILE), pl.ds(TILE * (m - 1), TILE)
            for c in range(chunks):
                backward = 1.0 / g[band, at(c)]
                inverse[c, own_band, :] = backward
                ratio[c, own_band, :] = share_v[own_band, at(c)] * backward
                slot = slot_v[own_band, at(c)]
                owner = slot // per_owner
                owner_v[c, own_band, :] = owner.astype(jnp.float32)
                spot_v[c, own_band, :] = (slot - owner * per_owner).astype(jnp.float32)
        for start in (*range(HALO + 1, HALO + rows - TILE, TILE), HALO + rows - TILE - 1):
            finish(start)
        lax.fori_loop(0, rows, make_hot, 0)

    @pl.when(me < n // 2)
    def _():
        local_work()

    pl.semaphore_wait(barrier, n - 1)
    own_land = land_recv.at[lax.rem(me, per_chunk), me // per_chunk]
    to_peers(0, lambda peer: land_send.at[peer], own_land)

    def halo_copy(i, up):
        src, dst = tall[i]
        if up:
            start, land, peer = (rows - half_way, HALO - half_way, me + 1)
        else:
            start, land, peer = (0, full - HALO, me - 1)
        return pltpu.make_async_remote_copy(
            src_ref=src.at[pl.ds(start, half_way)],
            dst_ref=dst.at[pl.ds(land, half_way)],
            send_sem=halo_sem.at[(0 if up else 1) + (0 if i in urgent else 12)],
            recv_sem=halo_sem.at[(2 if up else 3) + (0 if i in urgent else 12)],
            device_id={"tile": lax.rem(peer + n, n)},
            device_id_type=MESH,
        )

    def send_halo(which):
        @pl.when(me < n - 1)
        def _():
            for i in which:
                halo_copy(i, True).start()

        @pl.when(me > 0)
        def _():
            for i in which:
                halo_copy(i, False).start()

    send_halo(urgent)
    send_halo(patient)
    to_peers(1, lambda peer: slot_reach.at[peer // twins], places.at[me])
    land_recv[lax.rem(me, per_chunk), me // per_chunk] = land_send[me]

    @pl.when(me >= n // 2)
    def _():
        local_work()

    def take_halo(which):
        shift = 0 if which is urgent else 12
        size = water.at[:, pl.ds(0, len(which) * half_way), :]

        @pl.when(me > 0)
        def _():
            drain(size, halo_sem.at[2 + shift])

        @pl.when(me < n - 1)
        def _():
            drain(size, halo_sem.at[3 + shift])

    take_halo(urgent)
    outer = (0, full // TILE - 1)
    for m in outer:
        prepare_water(m)
    for start in (1, HALO + rows - 1):
        finish(start)

    drain(land_send.at[pl.ds(0, n - 1)], a2a_send.at[0])
    drain(land_send.at[pl.ds(0, n - 1)], a2a_recv.at[0])

    l_iota = lax.broadcasted_iota(jnp.int32, (LANES, 4 * LANES), 0)
    f_iota = lax.broadcasted_iota(jnp.int32, (LANES, 4 * LANES), 1)
    cell = lax.rem(f_iota, LANES) // 4
    group = f_iota // LANES
    total = None
    for k in range(per_chunk):
        inside = (cell >= k * cols) & (cell < (k + 1) * cols)
        spread = inside & (l_iota == group * cols + cell - k * cols)
        spread = jnp.where(spread, 1.0, 0.0).astype(jnp.bfloat16)
        block = land_recv[k].reshape(chunks * land_dev, LANES)
        for part in parts_of(block, 3):
            term = jnp.dot(part, spread, preferred_element_type=jnp.float32)
            total = term if total is None else total + term
    wide[...] = total

    def fill(m, i):
        band = pl.ds(TILE * m, TILE)
        for c in range(chunks):
            pair = []
            for q in (2 * m, 2 * m + 1):
                if q < side:
                    lanes, r = (2 + i) * LANES, q
                elif q < side + land_dev:
                    lanes, r = i * LANES, q - side
                else:
                    lanes, r = (2 + i) * LANES, q - land_dev
                r = c * land_dev + r
                pair.append(jnp.broadcast_to(wide[r : r + 1, lanes : lanes + LANES], (TILE, LANES)))
            added = jnp.where(top8, pair[0], pair[1])
            if i == 0:
                water[c, band, :] = g[band, at(c)] * (h[band, at(c)] + added)
            else:
                store[c, band, :] = s[band, at(c)] + added

    for m in (*outer, *inner):
        fill(m, 0)

    def advance_water(w, start, put):
        def load(c):
            wc = w[c, pl.ds(start, TILE), :]
            return (wc,) + rolled(wc)

        band, above, below = (pl.ds(start + q, TILE) for q in (0, -1, 1))
        before, here = (zero,) * 3, load(0)
        for c in range(chunks):
            after = load(c + 1) if c + 1 < chunks else (zero,) * 3
            flux = jnp.where(first, before[1], here[1]) + jnp.where(last, after[2], here[2])
            flux = flux + (w[c, above, :] + w[c, below, :])
            put(c, keep_h[c, band, :] * here[0] + square[c, band, :] * flux)
            before, here = here, after

    def advance_store(t, start, put):
        def load(c):
            tc = t[c, pl.ds(start, TILE), :]
            return (tc,) + rolled(tc)

        band, above, below = (pl.ds(start + q, TILE) for q in (0, -1, 1))
        before, here = (zero,) * 3, load(0)
        for c in range(chunks):
            after = load(c + 1) if c + 1 < chunks else (zero,) * 3
            moved = from_left[c, band, :] * jnp.where(first, before[1], here[1])
            moved = moved + from_right[c, band, :] * jnp.where(last, after[2], here[2])
            moved = moved + (down_v[c, above, :] * t[c, above, :] + up_v[c, below, :] * t[c, below, :])
            put(c, keep_s[c, band, :] * here[0] + moved)
            before, here = here, after

    top, end = HALO, HALO + rows
    later = ITERS - half_way - 1
    path = ((1, 0, 2), (4, 3, 5))

    def substep(advance, source, target, starts):
        for start in starts:

            def put(c, new):
                states[target][c, pl.ds(start, TILE), :] = new

            advance(states[source], start, put)

    def middle_copy(i, down):
        start = end - half_way if down else top
        return pltpu.make_async_remote_copy(
            src_ref=fields.at[path[i][0], :, pl.ds(start, half_way), :],
            dst_ref=middle.at[0 if down else 1, i],
            send_sem=halo_sem.at[4 + 2 * i + (0 if down else 1)],
            recv_sem=halo_sem.at[8 + 2 * i + (0 if down else 1)],
            device_id={"tile": lax.rem(me + (1 if down else n - 1), n)},
            device_id_type=MESH,
        )

    def first_half(i, advance):
        source, target = 3 * i, 3 * i + 1
        for reach in range(half_way - 1, 0, -1):
            substep(advance, source, target, range(top - reach, end + reach, TILE))
            source, target = target, source
        substep(advance, source, target, (top, end - TILE))

        @pl.when(me < n - 1)
        def _():
            middle_copy(i, True).start()

        @pl.when(me > 0)
        def _():
            middle_copy(i, False).start()

        substep(advance, source, target, range(top + TILE, end - TILE, TILE))

    def take_middle(i):
        @pl.when(me > 0)
        def _():
            middle_copy(i, True).wait_recv()

        @pl.when(me < n - 1)
        def _():
            middle_copy(i, False).wait_recv()

        for c in range(chunks):
            states[path[i][0]][c, top - half_way : top, :] = middle[0, i, c]
            states[path[i][0]][c, end : end + half_way, :] = middle[1, i, c]

    def edges(i, advance):
        for q in range(later):
            reach = later - q
            substep(advance, path[i][q], path[i][q + 1], (top - reach, end - TILE + reach))

    def last_water(starts):
        for start in starts:
            band = pl.ds(start - HALO, TILE)

            def put(c, new):
                final[c, band, :] = new
                taken = new * ratio[c, band, :]
                high = taken.astype(jnp.bfloat16).astype(jnp.float32)
                high_v[c, band, :] = high
                rest_v[c, band, :] = taken - high

            advance_water(states[path[0][later]], start, put)

    def last_store(starts):
        for start in starts:
            band = pl.ds(start - HALO, TILE)

            def put(c, new):
                sub_out[band, at(c)] = new

            advance_store(states[path[1][later]], start, put)

    first_half(0, advance_water)
    for q in range(later):
        reach = later - q
        substep(advance_water, path[0][q], path[0][q + 1], range(top + TILE - reach, end - TILE + reach, TILE))
    last_water(range(top + TILE, end - TILE, TILE))

    def add_row(r, total):
        hot = owner_hot[r]
        left = []
        for ref in (high_v, rest_v):
            row = jnp.concatenate([row_of(ref, c, r) for c in range(chunks)], axis=1)
            left += [hot[16 * q : 16 * (q + 1)] * row for q in range(n // 16)]
        left = jnp.concatenate(left, axis=0)
        return total + lax.dot_general(left, spot_hot[r], NT, preferred_element_type=jnp.float32)

    total = jnp.zeros((2 * n, per_owner), jnp.float32)
    total = lax.fori_loop(TILE, rows - TILE, add_row, total, unroll=8)
    take_middle(0)
    edges(0, advance_water)
    last_water((top, end - TILE))

    def add_wrapped(r, total):
        return add_row(lax.rem(r, rows), total)

    total = lax.fori_loop(rows - TILE, rows + TILE, add_wrapped, total, unroll=8)
    sums = total[:n] + total[n:]
    sums = jnp.concatenate([sums] * twins, axis=1)
    for k in range(n):
        sums_send[k] = sums[k : k + 1, :]
    sums_recv[me] = sums_send[me]
    to_peers(2, lambda peer: sums_send.at[peer], sums_recv.at[me])

    take_halo(patient)
    for m in outer:
        prepare_store(m)
    for m in (*outer, *inner):
        fill(m, 1)
    first_half(1, advance_store)
    for q in range(later):
        reach = later - q
        substep(advance_store, path[1][q], path[1][q + 1], range(top + TILE - reach, end - TILE + reach, TILE))
    last_store(range(top + TILE, end - TILE, TILE))
    for m in range(rows // TILE):
        band = pl.ds(TILE * m, TILE)
        for c in range(chunks):
            depth = final[c, band, :] * inverse[c, band, :]
            head_out[band, at(c)] = depth - share_v[band, at(c)] * depth

    drain(places.at[pl.ds(0, n - 1)], a2a_send.at[1])
    drain(places.at[pl.ds(0, n - 1)], a2a_recv.at[1])
    half = lax.broadcasted_iota(jnp.int32, (1, LANES), 1) // per_owner == lax.rem(me, twins)
    lane_line = lax.broadcasted_iota(jnp.int32, (LANES, LANES), 0)
    for j in range(n):
        low = lax.rem(places[j], LANES)
        spots[:, at(j)] = jnp.where(half & (lane_line == low), 1.0, 0.0).astype(jnp.bfloat16)

    take_middle(1)
    edges(1, advance_store)
    last_store((top, end - TILE))

    @pl.when(me < n - 1)
    def _():
        drain(water.at[:, pl.ds(0, len(urgent) * half_way), :], halo_sem.at[0])
        drain(water.at[:, pl.ds(0, len(patient) * half_way), :], halo_sem.at[12])
        middle_copy(0, True).wait_send()
        middle_copy(1, True).wait_send()

    @pl.when(me > 0)
    def _():
        drain(water.at[:, pl.ds(0, len(urgent) * half_way), :], halo_sem.at[1])
        drain(water.at[:, pl.ds(0, len(patient) * half_way), :], halo_sem.at[13])
        middle_copy(0, False).wait_send()
        middle_copy(1, False).wait_send()

    drain(sums_send.at[pl.ds(0, n - 1)], a2a_send.at[2])
    drain(sums_send.at[pl.ds(0, n - 1)], a2a_recv.at[2])


def flush(soil, head, sub, sums, places, spots, soil_out, head_out, sub_out, reach_out, reach_v, sem):
    copies = [
        pltpu.make_async_copy(src, dst, sem.at[i])
        for i, (src, dst) in enumerate(((head, head_out), (sub, sub_out), (soil, soil_out), (reach_v, reach_out)))
    ]
    for copy in copies[:-1]:
        copy.start()
    reach_rows = reach_v.shape[0]
    reach_line = lax.broadcasted_iota(jnp.int32, (reach_rows, LANES), 0)
    found = []
    for j in range(places.shape[0]):
        high = places[j] // LANES
        found.append(jnp.where(reach_line == high, sums[j], 0.0))
    found = jnp.concatenate(parts_of(jnp.concatenate(found, axis=1), 3), axis=0)
    reach = lax.dot_general(found, spots[...], NT, preferred_element_type=jnp.float32)
    reach_v[...] = reach[:reach_rows] + reach[reach_rows : 2 * reach_rows] + reach[2 * reach_rows :]
    copies[-1].start()
    for copy in copies:
        copy.wait()


def local(*args):
    n = lax.axis_size("tile")
    precip, head_init, slot_reach = args[0], args[5], args[12]
    cols, land_rows = precip.shape
    rows, width = head_init.shape
    slots = slot_reach.shape[0]
    full = rows + 2 * HALO
    land_dev = land_rows // n
    per_chunk = LANES // (width // n)
    chunks = width // LANES
    per_owner = slots // n
    f32, i32, b16 = jnp.float32, jnp.int32, jnp.bfloat16
    tall = pltpu.VMEM((full, width), f32)
    anywhere = pl.BlockSpec(memory_space=pl.ANY)
    results = pl.pallas_call(
        functools.partial(kernel, n),
        out_shape=(
            pltpu.VMEM(precip.shape, f32),
            pltpu.VMEM(head_init.shape, f32),
            pltpu.VMEM(head_init.shape, f32),
            pltpu.VMEM((n, 1, LANES), f32),
            pltpu.VMEM((n, 1, LANES), i32),
            pltpu.VMEM((LANES, n * LANES), b16),
        ),
        in_specs=[anywhere] * 13,
        out_specs=(pl.BlockSpec(memory_space=pltpu.VMEM),) * 6,
        scratch_shapes=[
            pltpu.VMEM((4, cols, land_rows), f32),
            pltpu.VMEM((cols, land_rows), i32),
            pltpu.VMEM((LANES, land_rows), f32),
            pltpu.VMEM((n, land_dev, LANES), f32),
            pltpu.VMEM((per_chunk, chunks, land_dev, LANES), f32),
            pltpu.VMEM((chunks * land_dev, 4 * LANES), f32),
            tall,
            tall,
            tall,
            tall,
            pltpu.VMEM((full, width), i32),
            pltpu.VMEM((rows, width), f32),
            pltpu.VMEM((rows, width), i32),
            pltpu.VMEM((6, chunks, full + TILE, LANES), f32),
            pltpu.VMEM((9, chunks, full + TILE, LANES), f32),
            pltpu.VMEM((chunks, rows, LANES), f32),
            pltpu.VMEM((chunks, rows, LANES), f32),
            pltpu.VMEM((chunks, rows, LANES), f32),
            pltpu.VMEM((2, chunks, rows + TILE, LANES), f32),
            pltpu.VMEM((2, chunks, rows + TILE, LANES), f32),
            pltpu.VMEM((rows, n, width), b16),
            pltpu.VMEM((rows, per_owner, width), b16),
            pltpu.VMEM((n, 1, LANES), f32),
            pltpu.VMEM((2, 2, chunks, ITERS // 2, LANES), f32),
            pltpu.SemaphoreType.DMA((2,)),
            pltpu.SemaphoreType.DMA((8,)),
            pltpu.SemaphoreType.DMA((16,)),
            pltpu.SemaphoreType.DMA((3,)),
            pltpu.SemaphoreType.DMA((3,)),
        ],
        compiler_params=pltpu.CompilerParams(
            collective_id=0,
            has_side_effects=True,
            vmem_limit_bytes=40 * 2**20,
        ),
        name="step",
    )(*[pltpu.with_memory_space_constraint(x, pltpu.HBM) for x in (*args[:12], slot_reach.reshape(slots // LANES, 1, LANES))])
    soil, head, sub, reach = pl.pallas_call(
        flush,
        out_shape=(
            *(jax.ShapeDtypeStruct(x.shape, x.dtype) for x in results[:3]),
            jax.ShapeDtypeStruct((slots // LANES, LANES), f32),
        ),
        in_specs=[pl.BlockSpec(memory_space=pltpu.VMEM)] * 6,
        out_specs=(anywhere,) * 4,
        scratch_shapes=[pltpu.VMEM((slots // LANES, LANES), f32), pltpu.SemaphoreType.DMA((4,))],
        compiler_params=pltpu.CompilerParams(vmem_limit_bytes=4 * 2**20),
        name="flush",
    )(*results)
    return soil, head, sub, reach.reshape(slots)


def solution(mesh):
    grid = P(("member", "tile"), None)
    line = P(("member", "tile"))
    return jax.shard_map(
        local,
        mesh=mesh,
        in_specs=(grid,) * 12 + (line,),
        out_specs=(grid, grid, grid, line),
        check_vma=False,
    )
```
